512 devices in a mesh: req: 128 (over z, y, core), tp: 4 (over x).
Axes of the slice: x: 4, y: 8, z: 8, core: 2. Of those that a mesh axis runs over, the one named last changes fastest.
Arguments:
- resid: bfloat16 [4096, 1536], P('req', 'tp'), may hold values from -2.5 to 2.5
- queries: bfloat16 [4096, 1536], P('req', 'tp'), may hold values from -250 to 250
- new_keys: bfloat16 [4096, 512], P('req', 'tp'), may hold values from -6 to 6
- new_values: bfloat16 [4096, 512], P('req', 'tp'), may hold values from -6 to 6
- k_cache: bfloat16 [4096, 128, 512], P('req', None, 'tp'), may hold values from -6.5 to 6.5
- v_cache: bfloat16 [4096, 128, 512], P('req', None, 'tp'), may hold values from -6 to 6
- lengths: int32 [4096], P('req'), may hold values from 2 to 128, as said below
- w_out: bfloat16 [1536, 1536], P('tp'), may hold values from -0.15625 to 0.15625
- norm_gain: float32 [1536], P('tp'), may hold values from 0.1 to 1.9
- w_router: float32 [1536, 16], P('tp'), may hold values from -0.08125 to 0.08125
- routes: int32 [4096, 2], P('req'), may hold values from 0 to 15, as said below
- w_gate: bfloat16 [128, 1536, 128], P('req', 'tp'), may hold values from -0.15625 to 0.15625
- w_up: bfloat16 [128, 1536, 128], P('req', 'tp'), may hold values from -0.15625 to 0.15625
- w_down: bfloat16 [128, 128, 1536], P('req', None, 'tp'), may hold values from -0.46875 to 0.46875
Outputs:
- attended: bfloat16 [4096, 1536], P('req', 'tp')
- layer_out: bfloat16 [4096, 1536], P('req', 'tp')
The draws below stay inside these ranges and needn't reach their ends.
Inputs may be any that keep to these rules, and one draw needn't show every extreme that they name: A request reads the first lengths[b] positions of its cache; some request has exactly 128, and some request exactly 2. `routes`: each request names two different experts; among the 32 requests of one device, at most 8 name the same expert, and on every device some expert is named exactly 8 times.
All inputs are finite; a program needn't handle non-finite values.
Results may differ from the reference program's by a relative error of at most 0.01.
Values may be sent and summed in bfloat16 or wider, within the bound.
A program may use at most 64 MiB of HBM per device.

```python
import math
import jax
import jax.numpy as jnp
from jax import lax

D = 1536
HEADS = 24
KV_HEADS = 8
HEAD_DIM = 64
FF = 1024
EXPERTS = 16
TOP = 2
REQ_DEV = 32
LMAX = 128
REQS = 4096
CAP = 8
SHARDS = 8
SLOTS = 128
FF_SH = 128
N_REQ = 128


def leading_keys(key):
    first_keys = jnp.clip(jax.random.normal(jax.random.fold_in(key, 11), (REQS, KV_HEADS * HEAD_DIM), jnp.float32), -6.0, 6.0)
    second_keys = jnp.clip(jax.random.normal(jax.random.fold_in(key, 12), (REQS, KV_HEADS * HEAD_DIM), jnp.float32), -6.0, 6.0)
    return (first_keys, second_keys)


def draw_k_cache(key, part):
    first_keys, second_keys = leading_keys(key)
    remaining = jnp.clip(jax.random.normal(jax.random.fold_in(key, 14), (REQS, LMAX - 2, KV_HEADS * HEAD_DIM), jnp.float32), -6.0, 6.0)
    stacked = jnp.concatenate([first_keys[:, None, :], second_keys[:, None, :], remaining], axis=1)
    return stacked.astype(jnp.bfloat16)


def draw_queries(key, part):
    drawn = jnp.clip(jax.random.normal(jax.random.fold_in(key, 21), (REQS, HEADS * HEAD_DIM), jnp.float32), -6.0, 6.0)
    return drawn.astype(jnp.bfloat16)


def column_profile():
    return jnp.exp(jnp.log(3.0) * jnp.arange(D, dtype=jnp.float32) / D)


def shared_direction(key):
    return jnp.clip(jax.random.normal(jax.random.fold_in(key, 61), (D,), jnp.float32), -4.0, 4.0)


def expert_levels(key):
    level_key = jax.random.fold_in(key, 71)
    ranking = jax.random.permutation(jax.random.fold_in(level_key, 1), EXPERTS)
    lower = ranking < EXPERTS // 4
    jitter = jax.random.uniform(jax.random.fold_in(level_key, 2), (EXPERTS,), jnp.float32, -0.25, 0.25)
    offset = jnp.where(lower, 0.0, 3.7) + jitter
    size_jitter = jax.random.uniform(jax.random.fold_in(level_key, 3), (EXPERTS,), jnp.float32, -0.2, 0.2)
    level = jnp.where(lower, 3.0, 0.12) * jnp.exp(size_jitter)
    return (offset, level)


def draw_resid(key, part):
    column_scale = column_profile()
    direction = shared_direction(key)
    noise_field = jnp.clip(jax.random.normal(jax.random.fold_in(key, 51), (REQS, D), jnp.float32), -6.0, 6.0)
    field = 0.12 * column_scale[None, :] * (direction[None, :] + 0.5 * noise_field)
    return jnp.clip(field, -2.5, 2.5).astype(jnp.bfloat16)


def draw_w_router(key, part):
    column_scale = column_profile()
    direction = shared_direction(key)
    offset, level = expert_levels(key)
    noise_part = jnp.clip(0.01 * jax.random.normal(jax.random.fold_in(key, 81), (D, EXPERTS), jnp.float32), -0.05, 0.05)
    aligned = (direction * column_scale)[:, None] * offset[None, :] / D
    return (noise_part + aligned).astype(jnp.float32)


def draw_w_down(key, part):
    offset, level = expert_levels(key)
    slot_expert = jnp.arange(SLOTS, dtype=jnp.int32) // SHARDS
    slot_scale = jnp.take(level, slot_expert) * FF ** (-0.5)
    base = jnp.clip(jax.random.normal(jax.random.fold_in(key, 91), (SLOTS, FF_SH, D), jnp.float32), -4.0, 4.0)
    return (base * slot_scale[:, None, None]).astype(jnp.bfloat16)


def draw_lengths(key, part):
    device_count = REQS // REQ_DEV
    halved_cap = jax.random.randint(jax.random.fold_in(key, 31), (device_count,), 0, 2)
    length_cap = jnp.repeat(jnp.where(halved_cap == 1, LMAX // 2, LMAX), REQ_DEV)
    lowest = jnp.maximum(length_cap // 4, 2)
    drawn_len = jax.random.randint(jax.random.fold_in(key, 32), (REQS,), lowest, length_cap + 1)
    chosen = jax.random.randint(jax.random.fold_in(key, 33), (), 0, REQS)
    offset = jax.random.randint(jax.random.fold_in(key, 34), (), 1, REQS)
    shortest = (chosen + offset) % REQS
    position = jnp.arange(REQS)
    drawn_len = jnp.where(position == shortest, 2, drawn_len)
    return jnp.where(position == chosen, LMAX, drawn_len).astype(jnp.int32)


def block_order(sub_key):
    return jax.random.permutation(sub_key, EXPERTS - 1)


def token_order(sub_key):
    return jax.random.permutation(sub_key, REQ_DEV)


def draw_routes(key, part):
    block_count = REQS // REQ_DEV
    route_count = REQ_DEV * TOP
    hot_expert = jax.random.randint(jax.random.fold_in(key, 41), (), 0, EXPERTS)
    orders = jax.vmap(block_order)(jax.random.split(jax.random.fold_in(key, 42), block_count)).astype(jnp.int32)
    others = orders + (orders >= hot_expert).astype(jnp.int32)
    ranked = jnp.concatenate([jnp.full((block_count, 1), hot_expert, jnp.int32), others], axis=1)
    full_count = jax.random.randint(jax.random.fold_in(key, 45), (block_count,), 2, 4).astype(jnp.int32)
    rank = jnp.arange(EXPERTS, dtype=jnp.int32)
    rest = route_count - full_count * CAP
    light_count = EXPERTS - full_count
    base = rest // light_count
    extra = rest % light_count
    beyond = rank[None, :] - full_count[:, None]
    counts = jnp.where(rank[None, :] < full_count[:, None], CAP, base[:, None] + (beyond < extra[:, None]).astype(jnp.int32))
    ends = jnp.cumsum(counts, axis=1)
    position = jnp.arange(route_count, dtype=jnp.int32)
    which = jnp.sum((position[None, :, None] >= ends[:, None, :]).astype(jnp.int32), axis=2)
    sequence = jnp.take_along_axis(ranked, which, axis=1)
    paired = jnp.stack([sequence[:, :REQ_DEV], sequence[:, REQ_DEV:]], axis=-1)
    flipped = jax.random.randint(jax.random.fold_in(key, 43), (block_count, REQ_DEV), 0, 2)
    paired = jnp.where(flipped[..., None] == 1, paired[..., ::-1], paired)
    shuffles = jax.vmap(token_order)(jax.random.split(jax.random.fold_in(key, 44), block_count)).astype(jnp.int32)
    paired = jnp.take_along_axis(paired, shuffles[..., None], axis=1)
    return paired.reshape(REQS, TOP).astype(jnp.int32)


def block_levels(rng, shape, pieces, least, top_value):
    level, own = 1.0, jax.random.fold_in(rng, 6)
    for dim, shards_of in pieces:
        draws = jnp.exp(jax.random.uniform(jax.random.fold_in(own, dim), (shards_of,), jnp.float32, least / len(pieces), top_value / len(pieces)))
        level = level * jnp.repeat(draws, shape[dim] // shards_of).reshape([-1 if axis == dim else 1 for axis in range(len(shape))])
    return level


def noise(own_key, extent, spread, most, cuts=(), kind=jnp.bfloat16):
    values = jax.random.normal(own_key, extent, jnp.float32) * spread
    if len(cuts) > 0:
        values = block_levels(own_key, extent, cuts, -0.22, 0.18) * values
    return jnp.clip(values, min=-most, max=most).astype(kind)


def setup_inputs(seed: int = 0) -> dict:
    keys = jax.random.split(jax.random.key(seed), 15)
    resid = draw_resid(jax.random.fold_in(keys[14], 71), 0)
    queries = draw_queries(jax.random.fold_in(keys[14], 71), 0)
    new_keys = noise(keys[2], (REQS, KV_HEADS * HEAD_DIM), 1.0, 6.0, ((0, 128), (1, 4)))
    new_values = noise(keys[3], (REQS, KV_HEADS * HEAD_DIM), 1.0, 6.0, ((0, 128), (1, 4)))
    k_cache = draw_k_cache(jax.random.fold_in(keys[14], 71), 0)
    v_cache = noise(keys[5], (REQS, LMAX, KV_HEADS * HEAD_DIM), 1.0, 6.0, ((0, 128), (2, 4)))
    lengths = draw_lengths(jax.random.fold_in(keys[14], 71), 0)
    w_out = noise(keys[7], (HEADS * HEAD_DIM, D), (HEADS * HEAD_DIM) ** -0.5, 0.15625, ((0, 4),))
    norm_gain = jnp.clip(1.0 + 0.18 * jax.random.normal(keys[8], (D,), jnp.float32), 0.1, 1.9)
    w_router = draw_w_router(jax.random.fold_in(keys[14], 71), 0)
    routes = draw_routes(jax.random.fold_in(keys[14], 71), 0)
    w_gate = noise(keys[11], (SLOTS, D, FF_SH), D ** -0.5, 0.15625, ((0, 128), (1, 4)))
    w_up = noise(keys[12], (SLOTS, D, FF_SH), D ** -0.5, 0.15625, ((0, 128), (1, 4)))
    w_down = draw_w_down(jax.random.fold_in(keys[14], 71), 0)
    return {"resid": resid, "queries": queries, "new_keys": new_keys, "new_values": new_values, "k_cache": k_cache, "v_cache": v_cache, "lengths": lengths, "w_out": w_out, "norm_gain": norm_gain, "w_router": w_router, "routes": routes, "w_gate": w_gate, "w_up": w_up, "w_down": w_down}


def attend_block(block_items):
    query_block, key_new, value_new, key_block, value_block, length_block = block_items
    row_count = query_block.shape[0]
    group_size = HEADS // KV_HEADS
    score_scale = 1.0 / math.sqrt(HEAD_DIM)
    query = query_block.astype(jnp.float32).reshape(row_count, KV_HEADS, group_size, HEAD_DIM)
    keys_all = key_block.astype(jnp.float32).reshape(row_count, LMAX, KV_HEADS, HEAD_DIM)
    values_all = value_block.astype(jnp.float32).reshape(row_count, LMAX, KV_HEADS, HEAD_DIM)
    scores = jnp.einsum('bgqd,blgd->bgql', query, keys_all) * score_scale
    self_score = jnp.einsum('bgqd,bgd->bgq', query, key_new.astype(jnp.float32).reshape(row_count, KV_HEADS, HEAD_DIM)) * score_scale
    valid_mask = (jnp.arange(LMAX, dtype=jnp.int32)[None, :] < length_block[:, None])[:, None, None, :]
    peak_score = jnp.maximum(lax.optimization_barrier(jnp.max(jnp.where(valid_mask, scores, -1e+30), axis=-1)), self_score)
    exp_terms = jnp.where(valid_mask, jnp.exp(scores - peak_score[..., None]), 0.0)
    self_exp = jnp.exp(self_score - peak_score)
    denom_sum = lax.optimization_barrier(jnp.sum(exp_terms, axis=-1)) + self_exp
    weights = (exp_terms / denom_sum[..., None]).astype(jnp.bfloat16)
    self_weight = (self_exp / denom_sum).astype(jnp.bfloat16)
    value_self = value_new.astype(jnp.float32).reshape(row_count, KV_HEADS, 1, HEAD_DIM)
    mixed = jnp.einsum('bgql,blgd->bgqd', weights.astype(jnp.float32), values_all) + self_weight.astype(jnp.float32)[..., None] * value_self
    return mixed.astype(jnp.bfloat16).reshape(row_count, HEADS * HEAD_DIM)

def reference(resid, queries, new_keys, new_values, k_cache, v_cache, lengths, w_out, norm_gain, w_router, routes, w_gate, w_up, w_down):
    block_count = REQS // REQ_DEV
    block_items = (queries.reshape(block_count, REQ_DEV, HEADS * HEAD_DIM), new_keys.reshape(block_count, REQ_DEV, KV_HEADS * HEAD_DIM), new_values.reshape(block_count, REQ_DEV, KV_HEADS * HEAD_DIM), k_cache.reshape(block_count, REQ_DEV, LMAX, KV_HEADS * HEAD_DIM), v_cache.reshape(block_count, REQ_DEV, LMAX, KV_HEADS * HEAD_DIM), lengths.reshape(block_count, REQ_DEV))
    attention = lax.map(attend_block, block_items).reshape(REQS, HEADS * HEAD_DIM)
    projected = jnp.dot(attention, w_out, preferred_element_type=jnp.float32)
    attended = (resid.astype(jnp.float32) + projected).astype(jnp.bfloat16)
    attended_f = attended.astype(jnp.float32)
    inv_rms = 1.0 / jnp.sqrt(lax.optimization_barrier(jnp.sum(attended_f * attended_f, axis=1)) / D + 1e-06)
    scaled = attended_f * norm_gain
    normed = (scaled * inv_rms[:, None]).astype(jnp.bfloat16)
    logits = jnp.dot(scaled, w_router, precision=lax.Precision.HIGHEST) * inv_rms[:, None]
    first_logit = jnp.take_along_axis(logits, routes[:, 0:1], axis=1)[:, 0]
    second_logit = jnp.take_along_axis(logits, routes[:, 1:2], axis=1)[:, 0]
    first_weight = jax.nn.sigmoid(first_logit - second_logit)
    second_weight = 1.0 - first_weight
    route_share = jnp.stack([first_weight, second_weight], axis=-1)
    gate_all = w_gate.reshape(EXPERTS, SHARDS, D, FF_SH).transpose(0, 2, 1, 3).reshape(EXPERTS, D, FF)
    up_all = w_up.reshape(EXPERTS, SHARDS, D, FF_SH).transpose(0, 2, 1, 3).reshape(EXPERTS, D, FF)
    down_all = w_down.reshape(EXPERTS, FF, D)
    most_rows = N_REQ * CAP

    def one_expert(accumulator, expert_items):
        gate_e, up_e, down_e, expert_index = expert_items
        matched = routes == expert_index
        share = lax.optimization_barrier(jnp.sum(jnp.where(matched, route_share, 0.0), axis=1))
        used_rows = jnp.any(matched, axis=1)
        used_count = jnp.sum(used_rows.astype(jnp.int32))
        picked = jnp.nonzero(used_rows, size=most_rows, fill_value=0)[0].astype(jnp.int32)
        picked_rows = normed[picked]
        gate_pre = jnp.dot(picked_rows, gate_e, preferred_element_type=jnp.float32)
        up_pre = jnp.dot(picked_rows, up_e, preferred_element_type=jnp.float32)
        hidden = (jax.nn.silu(gate_pre) * up_pre).astype(jnp.bfloat16)
        expert_out = jnp.dot(hidden, down_e, preferred_element_type=jnp.float32)
        keep_rows = jnp.arange(most_rows, dtype=jnp.int32) < used_count
        contrib = jnp.where(keep_rows[:, None], expert_out * share[picked][:, None], 0.0)
        return (accumulator.at[picked].add(contrib), None)
    moe, _unused = lax.scan(one_expert, jnp.zeros((REQS, D), jnp.float32), (gate_all, up_all, down_all, jnp.arange(EXPERTS, dtype=jnp.int32)))
    layer_out = (attended_f + moe).astype(jnp.bfloat16)
    return (attended, layer_out)
```

```python
import functools
import math

import jax
import jax.numpy as jnp
from jax import lax
from jax.experimental import pallas as pl
from jax.experimental.pallas import tpu as pltpu
from jax.sharding import PartitionSpec as P

HEAD_DIM = 64
CAP = 8
NZ = 8
NY = 8
MESH = pl.DeviceIdType.MESH
HIGHEST = lax.Precision.HIGHEST
F32 = jnp.float32
BF16 = jnp.bfloat16


def iota(shape, axis):
    return lax.broadcasted_iota(jnp.int32, shape, axis)


def shift_of(n):
    return int(math.log2(n))


def one_hot(mask, dtype=BF16):
    return jnp.where(mask, 1.0, 0.0).astype(dtype)


def dot(a, b, precision=None):
    return jnp.dot(a, b, preferred_element_type=F32, precision=precision)


def dot_nt(a, b, precision=None):
    return lax.dot_general(
        a, b, (((1,), (1,)), ((), ())), preferred_element_type=F32, precision=precision
    )


def attend(queries, new_keys, new_values, k_cache, v_cache, lens, rows):
    lanes = 2 * HEAD_DIM
    low = iota((rows, lanes), 1) < HEAD_DIM
    chunks = [queries[:, i * lanes : (i + 1) * lanes].astype(F32) for i in range(3)]
    turned = [pltpu.roll(chunks[0], HEAD_DIM, 1), None, pltpu.roll(chunks[2], HEAD_DIM, 1)]
    zero = jnp.zeros((rows, lanes), F32)
    heads = jnp.concatenate(
        [
            jnp.where(low, chunks[0], zero),
            jnp.where(low, turned[0], zero),
            jnp.where(low, chunks[1], zero),
            jnp.where(low, zero, chunks[1]),
            jnp.where(low, zero, turned[2]),
            jnp.where(low, zero, chunks[2]),
        ],
        axis=0,
    ).astype(BF16)
    log_rows = shift_of(rows)
    wide = (8 * rows, 6 * rows)
    i, j = iota(wide, 0), iota(wide, 1)
    spread = one_hot(((i >> 3) == (j & (rows - 1))) & ((i & 7) == (j >> log_rows)))
    query = dot(spread, heads)
    narrow = (8 * rows, rows)
    owner = one_hot((iota(narrow, 0) >> 3) == iota(narrow, 1))
    length = dot_nt(owner, jnp.broadcast_to(lens.astype(F32), (8, rows)).astype(BF16))[:, 0:1]
    key_self = dot(owner, new_keys)
    value_self = dot(owner, new_values)
    scale = 1.0 / math.sqrt(HEAD_DIM)
    cache_len = k_cache.shape[1]
    query3 = query.reshape(rows, 8, lanes).astype(BF16)
    scores = (
        jnp.einsum("bqd,bld->bql", query3, k_cache, preferred_element_type=F32) * scale
    ).reshape(8 * rows, cache_len)
    self_score = jnp.sum(query * key_self, axis=1, keepdims=True) * scale
    valid = iota((8 * rows, cache_len), 1).astype(F32) < length
    peak = jnp.maximum(
        jnp.max(jnp.where(valid, scores, -1e30), axis=1, keepdims=True), self_score
    )
    terms = jnp.where(valid, jnp.exp(scores - peak), 0.0)
    self_exp = jnp.exp(self_score - peak)
    total = jnp.sum(terms, axis=1, keepdims=True) + self_exp
    weights = (terms / total).reshape(rows, 8, cache_len).astype(BF16)
    self_weight = (self_exp / total).astype(BF16).astype(F32)
    mixed = jnp.einsum("bql,bld->bqd", weights, v_cache, preferred_element_type=F32)
    mixed = (mixed.reshape(8 * rows, lanes) + self_weight * value_self).astype(BF16)
    tall = (6 * rows, 8 * rows)
    i, j = iota(tall, 0), iota(tall, 1)
    gather = one_hot(((j >> 3) == (i & (rows - 1))) & ((j & 7) == (i >> log_rows)))
    out = dot(gather, mixed)
    head = [out[h * rows : (h + 1) * rows] for h in range(6)]
    return jnp.concatenate(
        [
            jnp.where(low, head[0], pltpu.roll(head[1], HEAD_DIM, 1)),
            jnp.where(low, head[2], head[3]),
            jnp.where(low, pltpu.roll(head[4], HEAD_DIM, 1), head[5]),
        ],
        axis=1,
    ).astype(BF16)


def kernel(
    nz,
    ny,
    nx,
    resid,
    queries,
    new_keys,
    new_values,
    k_cache,
    v_cache,
    lens,
    w_out,
    gain,
    router,
    routes,
    w_gate,
    w_up,
    w_down,
    att_out,
    layer_out,
    part_own,
    part_send,
    part_recv,
    gathered,
    gain_all,
    router_all,
    gate_up,
    down,
    rows_send,
    rows_recv,
    order_in,
    order_out,
    back_send,
    back_recv,
    moe_own,
    moe_send,
    moe_recv,
    own_sem,
    small_send,
    small_recv,
    part_ss,
    part_rs,
    gath_ss,
    gath_rs,
    near_ss,
    near_rs,
    far_ss,
    far_rs,
    core_ss,
    core_rs,
    disp_ss,
    disp_rs,
    back_ss,
    back_rs,
    moe_ss,
    moe_rs,
):
    rows, width = resid.shape
    depth = nx * width
    quad = ny // 2
    experts = 2 * nz
    chips = nz * ny
    per = CAP // nx
    units = w_gate.shape[1]
    req = lax.axis_index("req")
    x = lax.axis_index("tp")
    core = lax.rem(req, 2)
    chip = req // 2
    y = lax.rem(chip, ny)
    z = chip // ny

    def peer_x(step):
        return lax.rem(x + step, nx)

    def place(step):
        zz = lax.rem(z + step // ny, nz)
        yy = lax.rem(y + lax.rem(step, ny), ny)
        return zz, yy

    def device_of(zz, yy):
        return ((zz * ny + yy) * 2 + core, x)

    def remote(src, dst, ss, rs, device):
        return pltpu.make_async_remote_copy(
            src_ref=src, dst_ref=dst, send_sem=ss, recv_sem=rs, device_id=device,
            device_id_type=MESH,
        )

    barrier = pltpu.get_barrier_semaphore()

    @pl.loop(1, chips)
    def _(step):
        zz, yy = place(step)
        pl.semaphore_signal(barrier, inc=1, device_id=device_of(zz, yy), device_id_type=MESH)

    for step in range(1, nx):
        pl.semaphore_signal(barrier, inc=1, device_id=(req, peer_x(step)), device_id_type=MESH)
    partner = (req + 1 - 2 * core, x)
    pl.semaphore_signal(barrier, inc=1, device_id=partner, device_id_type=MESH)

    attention = attend(
        queries[...], new_keys[...], new_values[...], k_cache[...], v_cache[...], lens[...], rows
    )
    for f in range(nx):
        share = dot(attention, w_out[:, f * width : (f + 1) * width])
        part_own[f] = share
        part_send[f] = share.astype(BF16)

    pl.semaphore_wait(barrier, chips - 1 + nx)

    part_copies = []
    for step in range(1, nx):
        to = peer_x(step)
        copy = remote(
            part_send.at[to], part_recv.at[step - 1], part_ss.at[step - 1], part_rs.at[step - 1],
            (req, to),
        )
        copy.start()
        part_copies.append(copy)
    small = []
    for step in range(1, nx):
        to = peer_x(step)
        a = remote(gain, gain_all.at[x], small_send.at[0, step - 1], small_recv.at[0, step - 1], (req, to))
        b = remote(router, router_all.at[x], small_send.at[1, step - 1], small_recv.at[1, step - 1], (req, to))
        a.start()
        b.start()
        small += [a, b]

    def gate_at(xs, cc):
        return gate_up.at[pl.ds(pl.multiple_of(xs * width, width), width), pl.ds(pl.multiple_of(cc * units, units), units)]

    def up_at(xs, cc):
        return gate_up.at[
            pl.ds(pl.multiple_of(xs * width, width), width),
            pl.ds(pl.multiple_of(2 * units + cc * units, units), units),
        ]

    def down_at(xs, cc):
        return down.at[pl.ds(pl.multiple_of(cc * units, units), units), pl.ds(pl.multiple_of(xs * width, width), width)]

    places = (gate_at, up_at, down_at)
    mine = (w_gate, w_up, w_down)
    own = [
        pltpu.make_async_copy(mine[k], places[k](x, core), own_sem.at[k]) for k in range(3)
    ]
    own.append(pltpu.make_async_copy(gain, gain_all.at[x], own_sem.at[3]))
    own.append(pltpu.make_async_copy(router, router_all.at[x], own_sem.at[4]))
    for copy in own:
        copy.start()

    block = nx * per
    log_rows, log_per = shift_of(rows), shift_of(per)
    routes_f = jnp.broadcast_to(routes[0:1, :], (8, rows)), jnp.broadcast_to(routes[1:2, :], (8, rows))
    e_rows = iota((experts, rows), 0)
    names = one_hot((e_rows == routes[0:1, :]) | (e_rows == routes[1:2, :]), F32)
    before = one_hot(iota((rows, rows), 0) < iota((rows, rows), 1))
    rank = names * (dot(names.astype(BF16), before) + 1.0)
    tall = (experts * block, experts)
    lift = one_hot((iota(tall, 0) >> 3) == iota(tall, 1))
    flat = (rows, nx * rows)
    fan = one_hot(iota(flat, 0) == (iota(flat, 1) & (rows - 1)))
    value = dot(dot(lift, rank.astype(BF16)).astype(BF16), fan)
    full = (experts * block, nx * rows)
    i, j = iota(full, 0), iota(full, 1)
    wanted = (x * per + (i & (per - 1)) + 1).astype(F32)
    pick = one_hot((value == wanted) & (((i & 7) >> log_per) == (j >> log_rows)))

    eye = one_hot(iota((rows, rows), 0) == iota((rows, rows), 1))
    e_cols = iota((rows, experts), 1).astype(F32)
    first = one_hot(dot_nt(eye, routes_f[0].astype(F32).astype(BF16))[:, 0:1] == e_cols, F32)
    second = one_hot(dot_nt(eye, routes_f[1].astype(F32).astype(BF16))[:, 0:1] == e_cols, F32)
    earlier = one_hot(iota((rows, rows), 1) < iota((rows, rows), 0))
    count = dot(earlier, (first + second).astype(BF16)) + 1.0
    wide = (experts, experts * block)
    reach = one_hot(iota(wide, 0) == (iota(wide, 1) >> 3))
    back_full = (rows, experts * block)
    slot = iota(back_full, 1)
    target = (x * per + (slot & (per - 1)) + 1).astype(F32)
    slot_f = (slot & 7) >> log_per
    collect = []
    for marks in (first, second):
        held = dot((marks * count).astype(BF16), reach) == target
        for f in range(nx):
            collect.append(one_hot(held & (slot_f == f), F32))
    collect = jnp.concatenate(collect, axis=0)

    for copy in part_copies:
        copy.wait_recv()
    summed = resid[...].astype(F32) + part_own[x]
    for step in range(nx - 1):
        summed = summed + part_recv[step].astype(F32)
    attended = summed.astype(BF16)
    att_out[...] = attended
    gathered[x] = attended
    gath_copies = []
    for step in range(1, nx):
        to = peer_x(step)
        copy = remote(gathered.at[x], gathered.at[x], gath_ss.at[step - 1], gath_rs.at[step - 1], (req, to))
        copy.start()
        gath_copies.append(copy)

    near = (1, nx - 1) if nx > 2 else (1,)
    near_copies = {}
    for n, step in enumerate(near):
        for k in range(3):
            copy = remote(mine[k], places[k](x, core), near_ss.at[n, k], near_rs.at[n, k], (req, peer_x(step)))
            copy.start()
            near_copies[n, k] = copy

    for copy in own:
        copy.wait()
    for copy in small:
        copy.wait_recv()

    for copy in gath_copies:
        copy.wait_recv()
    att = [gathered[f].astype(F32) for f in range(nx)]
    square = jnp.sum(att[0] * att[0], axis=1, keepdims=True)
    for f in range(1, nx):
        square = square + jnp.sum(att[f] * att[f], axis=1, keepdims=True)
    inv_rms = 1.0 / jnp.sqrt(square / depth + 1e-06)
    scaled = [att[f] * gain_all[f] for f in range(nx)]
    normed = jnp.concatenate([(scaled[f] * inv_rms).astype(BF16) for f in range(nx)], axis=0)
    rows_send[...] = dot(pick, normed).reshape(experts, block, width).astype(BF16)

    here = z * ny + y
    keep = pltpu.make_async_copy(rows_send.at[2 * z + y // quad], rows_recv.at[here], disp_rs)
    keep.start()

    @pl.loop(1, chips)
    def _(step):
        zz, yy = place(step)
        remote(rows_send.at[2 * zz + yy // quad], rows_recv.at[here], disp_ss, disp_rs, device_of(zz, yy)).start()

    logits = dot_nt(scaled[0], router_all[0], HIGHEST)
    for f in range(1, nx):
        logits = logits + dot_nt(scaled[f], router_all[f], HIGHEST)
    logits = logits * inv_rms
    gap = jnp.sum(logits * first, axis=1, keepdims=True) - jnp.sum(
        logits * second, axis=1, keepdims=True
    )
    first_weight = jax.nn.sigmoid(gap)
    second_weight = 1.0 - first_weight

    total_rows = chips * block
    log_f = shift_of(chips * per)
    square_shape = (total_rows, total_rows)
    i, j = iota(square_shape, 0), iota(square_shape, 1)
    order_in[...] = one_hot(
        ((i >> log_f) == ((j & 7) >> log_per))
        & (((i & (chips * per - 1)) >> log_per) == (j >> 3))
        & ((i & (per - 1)) == (j & (per - 1)))
    )
    order_out[...] = one_hot(
        ((j >> log_f) == ((i & 7) >> log_per))
        & (((j & (chips * per - 1)) >> log_per) == (i >> 3))
        & ((j & (per - 1)) == (i & (per - 1)))
    )

    far_copies = []
    for copy in near_copies.values():
        copy.wait_recv()
    if nx > 2:
        left, right = peer_x(nx - 1), peer_x(1)
        half = units // 2

        def down_half(xs, top):
            return down.at[
                pl.ds(pl.multiple_of(core * units + top * half, half), half),
                pl.ds(pl.multiple_of(xs * width, width), width),
            ]

        moves = (
            (gate_at(left, core), right),
            (up_at(right, core), left),
            (down_half(left, 0), right),
            (down_half(right, 1), left),
        )
        for n, (ref, to) in enumerate(moves):
            copy = remote(ref, ref, far_ss.at[n], far_rs.at[n], (req, to))
            copy.start()
            far_copies.append(copy)
        for copy in far_copies:
            copy.wait_recv()

    core_copies = []
    shards = (
        gate_up.at[:, pl.ds(pl.multiple_of(core * units, units), units)],
        gate_up.at[:, pl.ds(pl.multiple_of(2 * units + core * units, units), units)],
        down.at[pl.ds(pl.multiple_of(core * units, units), units), :],
    )
    for k in range(3):
        copy = remote(shards[k], shards[k], core_ss.at[k], core_rs.at[k], partner)
        copy.start()
        core_copies.append(copy)

    remote(rows_recv, rows_recv, disp_ss, disp_rs, (req, x)).wait_recv()
    arrived = dot(order_in[...], rows_recv[...].reshape(total_rows, width)).astype(BF16)
    for copy in core_copies:
        copy.wait_recv()
    slots = chips * per
    both = dot(arrived[0:slots], gate_up[0:width, :])
    for f in range(1, nx):
        both = both + dot(arrived[f * slots : (f + 1) * slots], gate_up[f * width : (f + 1) * width, :])
    gate, up = both[:, : 2 * units], both[:, 2 * units :]
    hidden = (gate / (1.0 + jnp.exp(-gate)) * up).astype(BF16)
    outs = jnp.concatenate(
        [dot(hidden, down[:, f * width : (f + 1) * width]).astype(BF16) for f in range(nx)], axis=0
    )
    back_send[...] = dot(order_out[...], outs).reshape(chips, block, width).astype(BF16)

    keep_back = pltpu.make_async_copy(back_send.at[here], back_recv.at[here], back_rs)
    keep_back.start()

    @pl.loop(1, chips)
    def _(step):
        zz, yy = place(step)
        remote(back_send.at[zz * ny + yy], back_recv.at[here], back_ss, back_rs, device_of(zz, yy)).start()

    remote(back_recv, back_recv, back_ss, back_rs, (req, x)).wait_recv()
    came = back_recv[...].astype(F32).reshape(experts, quad, block, width)
    out_rows = came[:, 0]
    for k in range(1, quad):
        out_rows = out_rows + came[:, k]
    split = dot(collect, out_rows.reshape(experts * block, width), HIGHEST)
    for f in range(nx):
        moe = (
            first_weight * split[f * rows : (f + 1) * rows]
            + second_weight * split[(nx + f) * rows : (nx + f + 1) * rows]
        )
        moe_own[f] = moe
        moe_send[f] = moe.astype(BF16)
    moe_copies = []
    for step in range(1, nx):
        to = peer_x(step)
        copy = remote(moe_send.at[to], moe_recv.at[step - 1], moe_ss.at[step - 1], moe_rs.at[step - 1], (req, to))
        copy.start()
        moe_copies.append(copy)
    for copy in moe_copies:
        copy.wait_recv()
    moe = moe_own[x]
    for step in range(nx - 1):
        moe = moe + moe_recv[step].astype(F32)
    layer_out[...] = (att_out[...].astype(F32) + moe).astype(BF16)

    for copy in part_copies + small + gath_copies + list(near_copies.values()):
        copy.wait_send()
    for copy in far_copies + core_copies + moe_copies:
        copy.wait_send()
    rest = rows_recv.at[pl.ds(0, chips - 1)]
    remote(rest, rest, disp_ss, disp_rs, (req, x)).wait_send()
    rest = back_recv.at[pl.ds(0, chips - 1)]
    remote(rest, rest, back_ss, back_rs, (req, x)).wait_send()


def shards(nz, ny, nx, resid, queries, new_keys, new_values, k_cache, v_cache, lengths, w_out,
           norm_gain, w_router, routes, w_gate, w_up, w_down):
    rows, width = resid.shape
    units = w_gate.shape[2]
    chips, experts, block = nz * ny, 2 * nz, CAP
    total_rows = chips * block
    vmem, sem = pltpu.VMEM, pltpu.SemaphoreType.DMA
    out = jax.ShapeDtypeStruct((rows, width), BF16)
    return pl.pallas_call(
        functools.partial(kernel, nz, ny, nx),
        out_shape=(out, out),
        in_specs=[pl.BlockSpec(memory_space=pltpu.VMEM)] * 14,
        out_specs=[pl.BlockSpec(memory_space=pltpu.VMEM)] * 2,
        scratch_shapes=[
            vmem((nx, rows, width), F32),
            vmem((nx, rows, width), BF16),
            vmem((nx - 1, rows, width), BF16),
            vmem((nx, rows, width), BF16),
            vmem((nx, 1, width), F32),
            vmem((nx, experts, width), F32),
            vmem((nx * width, 4 * units), BF16),
            vmem((2 * units, nx * width), BF16),
            vmem((experts, block, width), BF16),
            vmem((chips, block, width), BF16),
            vmem((total_rows, total_rows), BF16),
            vmem((total_rows, total_rows), BF16),
            vmem((chips, block, width), BF16),
            vmem((chips, block, width), BF16),
            vmem((nx, rows, width), F32),
            vmem((nx, rows, width), BF16),
            vmem((nx - 1, rows, width), BF16),
            sem((5,)),
            sem((2, nx - 1)),
            sem((2, nx - 1)),
            sem((nx - 1,)),
            sem((nx - 1,)),
            sem((nx - 1,)),
            sem((nx - 1,)),
            sem((2, 3)),
            sem((2, 3)),
            sem((4,)),
            sem((4,)),
            sem((3,)),
            sem((3,)),
            sem(()),
            sem(()),
            sem(()),
            sem(()),
            sem((nx - 1,)),
            sem((nx - 1,)),
        ],
        compiler_params=pltpu.CompilerParams(
            collective_id=0, has_side_effects=True, vmem_limit_bytes=56 * 1024 * 1024
        ),
    )(
        resid, queries, new_keys, new_values, k_cache, v_cache, lengths.reshape(1, rows), w_out,
        norm_gain.reshape(1, width), w_router.T, routes.T, w_gate[0], w_up[0], w_down[0],
    )


def solution(mesh):
    nx = mesh.shape["tp"]
    nz = NZ
    ny = mesh.shape["req"] // (2 * nz)
    placed = (
        P("req", "tp"),
        P("req", "tp"),
        P("req", "tp"),
        P("req", "tp"),
        P("req", None, "tp"),
        P("req", None, "tp"),
        P("req"),
        P("tp", None),
        P("tp"),
        P("tp", None),
        P("req", None),
        P("req", "tp", None),
        P("req", "tp", None),
        P("req", None, "tp"),
    )
    return jax.shard_map(
        functools.partial(shards, nz, ny, nx),
        mesh=mesh,
        in_specs=placed,
        out_specs=(P("req", "tp"), P("req", "tp")),
        check_vma=False,
    )
```

```python
import functools
import math

import jax
import jax.numpy as jnp
from jax import lax
from jax.experimental import pallas as pl
from jax.experimental.pallas import tpu as pltpu
from jax.sharding import PartitionSpec as P

HEAD_DIM = 64
CAP = 8
NZ = 8
NY = 8
MESH = pl.DeviceIdType.MESH
HIGHEST = lax.Precision.HIGHEST
F32 = jnp.float32
BF16 = jnp.bfloat16


def iota(shape, axis):
    return lax.broadcasted_iota(jnp.int32, shape, axis)


def shift_of(n):
    return int(math.log2(n))


def one_hot(mask, dtype=BF16):
    return jnp.where(mask, 1.0, 0.0).astype(dtype)


def dot(a, b, precision=None):
    return jnp.dot(a, b, preferred_element_type=F32, precision=precision)


def dot_nt(a, b, precision=None):
    return lax.dot_general(
        a, b, (((1,), (1,)), ((), ())), preferred_element_type=F32, precision=precision
    )


def attend(queries_ref, new_keys_ref, new_values_ref, k_ref, v_ref, lens_ref, rows, ready):
    lanes = 2 * HEAD_DIM
    ready("queries")
    queries = queries_ref[...]
    low = iota((rows, lanes), 1) < HEAD_DIM
    chunks = [queries[:, i * lanes : (i + 1) * lanes].astype(F32) for i in range(3)]
    turned = [pltpu.roll(chunks[0], HEAD_DIM, 1), None, pltpu.roll(chunks[2], HEAD_DIM, 1)]
    zero = jnp.zeros((rows, lanes), F32)
    heads = jnp.concatenate(
        [
            jnp.where(low, chunks[0], zero),
            jnp.where(low, turned[0], zero),
            jnp.where(low, chunks[1], zero),
            jnp.where(low, zero, chunks[1]),
            jnp.where(low, zero, turned[2]),
            jnp.where(low, zero, chunks[2]),
        ],
        axis=0,
    ).astype(BF16)
    log_rows = shift_of(rows)
    wide = (8 * rows, 6 * rows)
    i, j = iota(wide, 0), iota(wide, 1)
    spread = one_hot(((i >> 3) == (j & (rows - 1))) & ((i & 7) == (j >> log_rows)))
    query = dot(spread, heads)
    narrow = (8 * rows, rows)
    owner = one_hot((iota(narrow, 0) >> 3) == iota(narrow, 1))
    ready("lens")
    lens = lens_ref[...]
    length = dot_nt(owner, jnp.broadcast_to(lens.astype(F32), (8, rows)).astype(BF16))[:, 0:1]
    ready("new_keys")
    ready("new_values")
    key_self = dot(owner, new_keys_ref[...])
    value_self = dot(owner, new_values_ref[...])
    scale = 1.0 / math.sqrt(HEAD_DIM)
    cache_len = k_ref.shape[1]
    ready("k_cache")
    query3 = query.reshape(rows, 8, lanes).astype(BF16)
    scores = (
        jnp.einsum("bqd,bld->bql", query3, k_ref[...], preferred_element_type=F32) * scale
    ).reshape(8 * rows, cache_len)
    self_score = jnp.sum(query * key_self, axis=1, keepdims=True) * scale
    valid = iota((8 * rows, cache_len), 1).astype(F32) < length
    peak = jnp.maximum(
        jnp.max(jnp.where(valid, scores, -1e30), axis=1, keepdims=True), self_score
    )
    terms = jnp.where(valid, jnp.exp(scores - peak), 0.0)
    self_exp = jnp.exp(self_score - peak)
    total = jnp.sum(terms, axis=1, keepdims=True) + self_exp
    weights = (terms / total).reshape(rows, 8, cache_len).astype(BF16)
    self_weight = (self_exp / total).astype(BF16).astype(F32)
    ready("v_cache")
    mixed = jnp.einsum("bql,bld->bqd", weights, v_ref[...], preferred_element_type=F32)
    mixed = (mixed.reshape(8 * rows, lanes) + self_weight * value_self).astype(BF16)
    tall = (6 * rows, 8 * rows)
    i, j = iota(tall, 0), iota(tall, 1)
    gather = one_hot(((j >> 3) == (i & (rows - 1))) & ((j & 7) == (i >> log_rows)))
    out = dot(gather, mixed)
    head = [out[h * rows : (h + 1) * rows] for h in range(6)]
    return jnp.concatenate(
        [
            jnp.where(low, head[0], pltpu.roll(head[1], HEAD_DIM, 1)),
            jnp.where(low, head[2], head[3]),
            jnp.where(low, pltpu.roll(head[4], HEAD_DIM, 1), head[5]),
        ],
        axis=1,
    ).astype(BF16)


INPUTS = [
    "resid", "queries", "new_keys", "new_values", "k_cache", "v_cache", "lens", "w_out", "gain",
    "router", "routes", "gate", "up", "down",
]
HELD = [name for name in INPUTS if name not in ("gain", "router", "gate", "up", "down")]
LOADS = [
    "queries", "k_cache", "lens", "new_keys", "new_values", "v_cache", "w_out", "gain", "gate",
    "up", "down", "resid", "routes", "router",
]


def group_of(chips, ny):
    return min(chips, 2 * ny)


def plan(nz, ny, nx, rows, width, units, shapes):
    vmem, dma = pltpu.VMEM, pltpu.SemaphoreType.DMA
    chips, experts, block = nz * ny, 2 * nz, CAP
    near = min(2, nx - 1)
    out = {name + "_v": vmem(shapes[name].shape, shapes[name].dtype) for name in HELD}
    out.update(
        part_own=vmem((nx, rows, width), F32),
        part_send=vmem((nx, rows, width), BF16),
        part_recv=vmem((nx - 1, rows, width), BF16),
        gathered=vmem((nx, rows, width), BF16),
        gain_all=vmem((nx,) + shapes["gain"].shape, F32),
        router_all=vmem((nx, experts, width), F32),
        gate_up=vmem((nx, 2, 2, width, units), BF16),
        down_all=vmem((nx, 2, units, width), BF16),
        rows_send=vmem((experts, block, width), BF16),
        rows_recv=vmem((chips, block, width), BF16),
        back_send=vmem((chips, block, width), BF16),
        back_recv=vmem((chips, block, width), BF16),
        moe_own=vmem((nx, rows, width), F32),
        moe_send=vmem((nx, rows, width), BF16),
        moe_recv=vmem((nx - 1, rows, width), BF16),
        load_sem=dma((len(INPUTS),)),
        line_sem=pltpu.SemaphoreType.REGULAR,
        gain_ss=dma((nx - 1,)),
        gain_rs=dma((nx - 1,)),
        router_ss=dma((nx - 1,)),
        router_rs=dma((nx - 1,)),
        part_ss=dma((nx - 1,)),
        part_rs=dma((nx - 1,)),
        gath_ss=dma((nx - 1,)),
        gath_rs=dma((nx - 1,)),
        near_ss=dma((near, 3)),
        near_rs=dma((near, 3)),
        far_ss=dma((4,)),
        far_rs=dma((4,)),
        core_ss=dma((nx, 2)),
        core_rs=dma((nx, 2)),
        disp_ss=dma(()),
        disp_rs=dma((chips // group_of(chips, ny),)),
        back_ss=dma(()),
        back_rs=dma(()),
        moe_ss=dma((nx - 1,)),
        moe_rs=dma((nx - 1,)),
    )
    return out


class Refs:
    pass


def kernel(nz, ny, nx, names, *args):
    r = Refs()
    for name, ref in zip(names, args):
        setattr(r, name, ref)
    rows, width = r.resid.shape
    depth = nx * width
    quad = ny // 2
    experts = 2 * nz
    chips = nz * ny
    per = CAP // nx
    units = r.gate.shape[1]
    req = lax.axis_index("req")
    x = lax.axis_index("tp")
    core = lax.rem(req, 2)
    chip = req // 2
    y = lax.rem(chip, ny)
    z = chip // ny
    here = z * ny + y
    partner = (req + 1 - 2 * core, x)

    def peer_x(step):
        return lax.rem(x + step, nx)

    def device_of(zz, yy):
        return ((zz * ny + yy) * 2 + core, x)

    def far_first(size):
        return sorted(range(size), key=lambda d: (-min(d, size - d), d))

    def far_apart():
        def key(offset):
            hops = [min(d, n - d) for d, n in zip(offset, (nz, ny))]
            return -sum(hops), hops[0], sum(d > n // 2 for d, n in zip(offset, (nz, ny))) % 2, offset

        return sorted(((a, b) for a in range(nz) for b in range(ny) if a or b), key=key)

    def remote(src, dst, ss, rs, device):
        return pltpu.make_async_remote_copy(
            src_ref=src, dst_ref=dst, send_sem=ss, recv_sem=rs, device_id=device,
            device_id_type=MESH,
        )

    def gate_at(xs):
        return r.gate_up.at[xs, core, 0]

    def up_at(xs):
        return r.gate_up.at[xs, core, 1]

    def down_at(xs):
        return r.down_all.at[xs, core]

    places = (gate_at, up_at, down_at)

    targets = dict(
        gain=r.gain_all.at[x], router=r.router_all.at[x], gate=gate_at(x), up=up_at(x),
        down=down_at(x),
    )
    loads = {}
    for name in LOADS:
        target = targets[name] if name in targets else getattr(r, name + "_v")
        sem = r.load_sem.at[INPUTS.index(name)]
        loads[name] = pltpu.make_async_copy(getattr(r, name), target, sem)
        loads[name].start()

    def ready(name):
        loads[name].wait()

    barrier = pltpu.get_barrier_semaphore()

    def greet(device):
        pl.semaphore_signal(barrier, inc=1, device_id=device, device_id_type=MESH)

    for step in range(1, nx):
        greet((req, peer_x(step)))
    greet(partner)
    line_y = [device_of(z, lax.rem(y + d, ny)) for d in far_first(ny) if d]
    line_z = [device_of(lax.rem(z + d, nz), y) for d in far_first(nz) if d]
    for device in line_y + line_z:
        greet(device)

    attention = attend(
        r.queries_v, r.new_keys_v, r.new_values_v, r.k_cache_v, r.v_cache_v, r.lens_v, rows, ready
    )
    ready("w_out")
    for f in range(nx):
        share = dot(attention, r.w_out_v[:, f * width : (f + 1) * width])
        r.part_own[f] = share
        r.part_send[f] = share.astype(BF16)

    ready("gain")
    pl.semaphore_wait(barrier, nx + (ny - 1) + (nz - 1))

    part_copies, gain_copies = [], []
    for step in range(1, nx):
        n, to = step - 1, peer_x(step)
        part_copies.append(
            remote(r.part_send.at[to], r.part_recv.at[n], r.part_ss.at[n], r.part_rs.at[n], (req, to))
        )
        part_copies[n].start()
    for step in range(1, nx):
        n, to = step - 1, peer_x(step)
        gain_copies.append(
            remote(r.gain_all.at[x], r.gain_all.at[x], r.gain_ss.at[n], r.gain_rs.at[n], (req, to))
        )
        gain_copies[n].start()

    for name in ("gate", "up", "down"):
        ready(name)
    near = (1, nx - 1) if nx > 2 else (1,)
    near_copies = {
        (n, k): remote(
            places[k](x), places[k](x), r.near_ss.at[n, k], r.near_rs.at[n, k],
            (req, peer_x(step)),
        )
        for k in range(3)
        for n, step in enumerate(near)
    }

    def core_send(step, k):
        xs = peer_x(step)
        ref = r.down_all.at[xs, core] if k else r.gate_up.at[xs, core]
        copy = remote(ref, ref, r.core_ss.at[step, k], r.core_rs.at[step, k], partner)
        copy.start()
        return copy

    for n in range(len(near)):
        near_copies[n, 0].start()
    core_copies = [core_send(0, k) for k in range(2)]

    for device in line_z:
        pl.semaphore_signal(r.line_sem, inc=1, device_id=device, device_id_type=MESH)

    ready("routes")
    routes = r.routes_v[...]
    block = nx * per
    log_rows, log_per = shift_of(rows), shift_of(per)
    e_rows = iota((experts, rows), 0)
    names_e = one_hot((e_rows == routes[0:1, :]) | (e_rows == routes[1:2, :]), F32)
    before = one_hot(iota((rows, rows), 0) < iota((rows, rows), 1))
    rank = names_e * (dot(names_e.astype(BF16), before) + 1.0)
    tall = (experts * block, experts)
    lift = one_hot((iota(tall, 0) >> 3) == iota(tall, 1))
    flat = (rows, nx * rows)
    fan = one_hot(iota(flat, 0) == (iota(flat, 1) & (rows - 1)))
    value = dot(dot(lift, rank.astype(BF16)).astype(BF16), fan)
    full = (experts * block, nx * rows)
    i, j = iota(full, 0), iota(full, 1)
    wanted = (x * per + (i & (per - 1)) + 1).astype(F32)
    pick = one_hot((value == wanted) & (((i & 7) >> log_per) == (j >> log_rows)))

    eye = one_hot(iota((rows, rows), 0) == iota((rows, rows), 1))
    e_cols = iota((rows, experts), 1).astype(F32)

    def column(k):
        row = jnp.broadcast_to(routes[k : k + 1, :], (8, rows)).astype(F32).astype(BF16)
        return dot_nt(eye, row)[:, 0:1]

    first = one_hot(column(0) == e_cols, F32)
    second = one_hot(column(1) == e_cols, F32)
    earlier = one_hot(iota((rows, rows), 1) < iota((rows, rows), 0))
    count = dot(earlier, (first + second).astype(BF16)) + 1.0
    wide = (experts, experts * block)
    reach = one_hot(iota(wide, 0) == (iota(wide, 1) >> 3))
    slot = iota((rows, experts * block), 1)
    target = (x * per + (slot & (per - 1)) + 1).astype(F32)
    slot_f = (slot & 7) >> log_per
    collect = []
    for marks in (first, second):
        held = dot((marks * count).astype(BF16), reach) == target
        for f in range(nx):
            collect.append(one_hot(held & (slot_f == f), F32))
    collect = jnp.concatenate(collect, axis=0)

    group = group_of(chips, ny)
    batch = group * block
    log_f = shift_of(group * per)
    i, j = iota((batch, batch), 0), iota((batch, batch), 1)

    def same_row(a, b):
        return one_hot(
            ((a >> log_f) == ((b & 7) >> log_per))
            & (((a & (group * per - 1)) >> log_per) == (b >> 3))
            & ((a & (per - 1)) == (b & (per - 1)))
        )

    order_in, order_out = same_row(i, j), same_row(j, i)

    ready("resid")
    for copy in part_copies:
        copy.wait_recv()
    summed = r.resid_v[...].astype(F32) + r.part_own[x]
    for n in range(nx - 1):
        summed = summed + r.part_recv[n].astype(F32)
    attended = summed.astype(BF16)
    r.gathered[x] = attended
    gath_copies = []
    for step in range(1, nx):
        n, to = step - 1, peer_x(step)
        gath_copies.append(
            remote(r.gathered.at[x], r.gathered.at[x], r.gath_ss.at[n], r.gath_rs.at[n], (req, to))
        )
        gath_copies[n].start()
    for k in (1, 2):
        for n in range(len(near)):
            near_copies[n, k].start()
    ready("router")
    router_copies = []
    for step in range(1, nx):
        n, to = step - 1, peer_x(step)
        router_copies.append(
            remote(r.router_all.at[x], r.router_all.at[x], r.router_ss.at[n], r.router_rs.at[n], (req, to))
        )
        router_copies[n].start()
    r.att_out[...] = attended
    pl.semaphore_wait(r.line_sem, nz - 1)
    for copy in gain_copies:
        copy.wait_recv()
    gains = [
        jnp.concatenate([r.gain_all[f, k : k + 1, :] for k in range(width // 128)], axis=1)
        for f in range(nx)
    ]

    for copy in gath_copies:
        copy.wait_recv()
    left, right = peer_x(nx - 1), peer_x(1)
    far_copies = []

    def pass_far(ref, to):
        n = len(far_copies)
        far_copies.append(remote(ref, ref, r.far_ss.at[n], r.far_rs.at[n], (req, to)))
        far_copies[n].start()

    for n in range(len(near)):
        near_copies[n, 0].wait_recv()
    if nx > 2:
        pass_far(gate_at(left), right)

    att = [r.gathered[f].astype(F32) for f in range(nx)]
    square = jnp.sum(att[0] * att[0], axis=1, keepdims=True)
    for f in range(1, nx):
        square = square + jnp.sum(att[f] * att[f], axis=1, keepdims=True)
    inv_rms = 1.0 / jnp.sqrt(square / depth + 1e-06)
    scaled = [att[f] * gains[f] for f in range(nx)]
    normed = jnp.concatenate([(scaled[f] * inv_rms).astype(BF16) for f in range(nx)], axis=0)
    r.rows_send[...] = dot(pick, normed).reshape(experts, block, width).astype(BF16)

    plane = z // (group // ny)
    for dz, dy in far_apart():
        zz, yy = lax.rem(z + dz, nz), lax.rem(y + dy, ny)
        remote(
            r.rows_send.at[2 * zz + yy // quad], r.rows_recv.at[here], r.disp_ss,
            r.disp_rs.at[plane], device_of(zz, yy),
        ).start()
    keep = pltpu.make_async_copy(
        r.rows_send.at[2 * z + y // quad], r.rows_recv.at[here], r.disp_rs.at[plane]
    )
    keep.start()

    half = units // 2
    for n in range(len(near)):
        near_copies[n, 1].wait_recv()
    if nx > 2:
        pass_far(up_at(right), left)
    core_copies += [core_send(step, 0) for step in near]
    for n in range(len(near)):
        near_copies[n, 2].wait_recv()
    if nx > 2:
        pass_far(r.down_all.at[left, core, pl.ds(0, half)], right)
        pass_far(r.down_all.at[right, core, pl.ds(half, half)], left)
    core_copies += [core_send(step, 1) for step in near]

    for copy in router_copies:
        copy.wait_recv()
    logits = dot_nt(scaled[0], r.router_all[0], HIGHEST)
    for f in range(1, nx):
        logits = logits + dot_nt(scaled[f], r.router_all[f], HIGHEST)
    logits = logits * inv_rms
    gap = jnp.sum(logits * first, axis=1, keepdims=True) - jnp.sum(
        logits * second, axis=1, keepdims=True
    )
    first_weight = jax.nn.sigmoid(gap)
    second_weight = 1.0 - first_weight

    if nx > 2:
        for copy in far_copies[:2]:
            copy.wait_recv()
        core_copies.append(core_send(2, 0))
        for copy in far_copies[2:]:
            copy.wait_recv()
        core_copies.append(core_send(2, 1))

    groups = range(chips // group)
    lot = group * per
    arrived = []
    for g in groups:
        part = r.rows_recv.at[pl.ds(g * group, group)]
        remote(part, part, r.disp_ss, r.disp_rs.at[g], (req, x)).wait_recv()
        arrived.append(dot(order_in, part[...].reshape(batch, width)).astype(BF16))
    for copy in core_copies:
        copy.wait_recv()
    both = None
    for f in range(nx):
        lhs = jnp.concatenate([a[f * lot : (f + 1) * lot] for a in arrived], axis=0)
        rhs = jnp.concatenate(
            [r.gate_up[f, c, k] for k in range(2) for c in range(2)], axis=1
        )
        both = dot(lhs, rhs) if f == 0 else both + dot(lhs, rhs)
    gate, up = both[:, : 2 * units], both[:, 2 * units :]
    hidden = (gate / (1.0 + jnp.exp(-gate)) * up).astype(BF16)
    outs = [
        dot(hidden, jnp.concatenate([r.down_all[f, c] for c in range(2)], axis=0)).astype(BF16)
        for f in range(nx)
    ]

    for g in groups:
        stack = jnp.concatenate([out[g * lot : (g + 1) * lot] for out in outs], axis=0)
        r.back_send[g * group : (g + 1) * group] = (
            dot(order_out, stack).reshape(group, block, width).astype(BF16)
        )
        for zz in range(g * (group // ny), (g + 1) * (group // ny)):
            for dy in far_first(ny):
                yy = lax.rem(y + dy, ny)

                def send():
                    remote(
                        r.back_send.at[zz * ny + yy], r.back_recv.at[here], r.back_ss, r.back_rs,
                        device_of(zz, yy),
                    ).start()

                if dy:
                    send()
                else:
                    pl.when(zz != z)(send)
    keep_back = pltpu.make_async_copy(r.back_send.at[here], r.back_recv.at[here], r.back_rs)
    keep_back.start()

    remote(r.back_recv, r.back_recv, r.back_ss, r.back_rs, (req, x)).wait_recv()
    came = r.back_recv[...].astype(F32).reshape(experts, quad, block, width)
    out_rows = came[:, 0]
    for k in range(1, quad):
        out_rows = out_rows + came[:, k]
    split = dot(collect, out_rows.reshape(experts * block, width), HIGHEST)
    for f in range(nx):
        moe = (
            first_weight * split[f * rows : (f + 1) * rows]
            + second_weight * split[(nx + f) * rows : (nx + f + 1) * rows]
        )
        r.moe_own[f] = moe
        r.moe_send[f] = moe.astype(BF16)
    moe_copies = []
    for step in range(1, nx):
        n, to = step - 1, peer_x(step)
        moe_copies.append(
            remote(r.moe_send.at[to], r.moe_recv.at[n], r.moe_ss.at[n], r.moe_rs.at[n], (req, to))
        )
        moe_copies[n].start()

    for copy in part_copies + gain_copies + gath_copies + router_copies:
        copy.wait_send()
    for copy in list(near_copies.values()) + far_copies + core_copies:
        copy.wait_send()
    rest = r.rows_recv.at[pl.ds(0, chips - 1)]
    remote(rest, rest, r.disp_ss, r.disp_rs, (req, x)).wait_send()
    rest = r.back_recv.at[pl.ds(0, chips - 1)]
    remote(rest, rest, r.back_ss, r.back_rs, (req, x)).wait_send()

    for copy in moe_copies:
        copy.wait_recv()
    moe = r.moe_own[x]
    for n in range(nx - 1):
        moe = moe + r.moe_recv[n].astype(F32)
    r.layer_out[...] = (attended.astype(F32) + moe).astype(BF16)
    for copy in moe_copies:
        copy.wait_send()


def pass_on(a_in, b_in, a_out, b_out):
    a_out[...] = a_in[...]
    b_out[...] = b_in[...]


def shards(nz, ny, nx, resid, queries, new_keys, new_values, k_cache, v_cache, lengths, w_out,
           norm_gain, w_router, routes, w_gate, w_up, w_down):
    rows, width = resid.shape
    units = w_gate.shape[2]
    operands = (
        resid, queries, new_keys, new_values, k_cache, v_cache, lengths.reshape(1, rows), w_out,
        norm_gain.reshape(width // 128, 128), w_router.T, routes.T, w_gate[0], w_up[0], w_down[0],
    )
    scratch = plan(nz, ny, nx, rows, width, units, dict(zip(INPUTS, operands)))
    names = INPUTS + ["att_out", "layer_out"] + list(scratch)
    out = jax.ShapeDtypeStruct((rows, width), BF16)
    whole = pl.BlockSpec(memory_space=pltpu.VMEM)
    results = pl.pallas_call(
        functools.partial(kernel, nz, ny, nx, names),
        out_shape=(pltpu.VMEM((rows, width), BF16),) * 2,
        in_specs=[pl.BlockSpec(memory_space=pl.ANY)] * len(operands),
        out_specs=[whole] * 2,
        scratch_shapes=list(scratch.values()),
        compiler_params=pltpu.CompilerParams(
            collective_id=0, has_side_effects=True, vmem_limit_bytes=56 * 1024 * 1024
        ),
    )(*operands)
    return pl.pallas_call(
        pass_on, out_shape=(out, out), in_specs=[whole] * 2, out_specs=[whole] * 2
    )(*(pltpu.with_memory_space_constraint(a, pltpu.VMEM) for a in results))


def solution(mesh):
    nx = mesh.shape["tp"]
    nz = NZ
    ny = mesh.shape["req"] // (2 * nz)
    placed = (
        P("req", "tp"),
        P("req", "tp"),
        P("req", "tp"),
        P("req", "tp"),
        P("req", None, "tp"),
        P("req", None, "tp"),
        P("req"),
        P("tp", None),
        P("tp"),
        P("tp", None),
        P("req", None),
        P("req", "tp", None),
        P("req", "tp", None),
        P("req", None, "tp"),
    )
    return jax.shard_map(
        functools.partial(shards, nz, ny, nx),
        mesh=mesh,
        in_specs=placed,
        out_specs=(P("req", "tp"), P("req", "tp")),
        check_vma=False,
    )
```

```python
import functools
import math

import jax
import jax.numpy as jnp
from jax import lax
from jax.experimental import pallas as pl
from jax.experimental.pallas import tpu as pltpu
from jax.sharding import PartitionSpec as P

HEAD_DIM = 64
CAP = 8
NZ = 8
NY = 8
PLANES = 2
MESH = pl.DeviceIdType.MESH
HIGHEST = lax.Precision.HIGHEST
F32 = jnp.float32
BF16 = jnp.bfloat16


def iota(shape, axis):
    return lax.broadcasted_iota(jnp.int32, shape, axis)


def shift_of(n):
    return int(math.log2(n))


def one_hot(mask, dtype=BF16):
    return jnp.where(mask, 1.0, 0.0).astype(dtype)


def dot(a, b, precision=None):
    return jnp.dot(a, b, preferred_element_type=F32, precision=precision)


def dot_nt(a, b, precision=None):
    return lax.dot_general(
        a, b, (((1,), (1,)), ((), ())), preferred_element_type=F32, precision=precision
    )


def attend(queries_ref, new_keys_ref, new_values_ref, k_ref, v_ref, lens_ref, rows, ready, meanwhile):
    lanes = 2 * HEAD_DIM
    ready("queries")
    queries = queries_ref[...]
    low = iota((rows, lanes), 1) < HEAD_DIM
    chunks = [queries[:, i * lanes : (i + 1) * lanes].astype(F32) for i in range(3)]
    turned = [pltpu.roll(chunks[0], HEAD_DIM, 1), None, pltpu.roll(chunks[2], HEAD_DIM, 1)]
    zero = jnp.zeros((rows, lanes), F32)
    heads = jnp.concatenate(
        [
            jnp.where(low, chunks[0], zero),
            jnp.where(low, turned[0], zero),
            jnp.where(low, chunks[1], zero),
            jnp.where(low, zero, chunks[1]),
            jnp.where(low, zero, turned[2]),
            jnp.where(low, zero, chunks[2]),
        ],
        axis=0,
    ).astype(BF16)
    log_rows = shift_of(rows)
    wide = (8 * rows, 6 * rows)
    i, j = iota(wide, 0), iota(wide, 1)
    spread = one_hot(((i >> 3) == (j & (rows - 1))) & ((i & 7) == (j >> log_rows)))
    query = dot(spread, heads)
    narrow = (8 * rows, rows)
    owner = one_hot((iota(narrow, 0) >> 3) == iota(narrow, 1))
    ready("lens")
    lens = lens_ref[...]
    length = dot_nt(owner, jnp.broadcast_to(lens.astype(F32), (8, rows)).astype(BF16))[:, 0:1]
    ready("new_keys")
    ready("new_values")
    key_self = dot(owner, new_keys_ref[...])
    value_self = dot(owner, new_values_ref[...])
    scale = 1.0 / math.sqrt(HEAD_DIM)
    cache_len = k_ref.shape[1]
    meanwhile()
    ready("k_cache")
    query3 = query.reshape(rows, 8, lanes).astype(BF16)
    scores = (
        jnp.einsum("bqd,bld->bql", query3, k_ref[...], preferred_element_type=F32) * scale
    ).reshape(8 * rows, cache_len)
    self_score = jnp.sum(query * key_self, axis=1, keepdims=True) * scale
    valid = iota((8 * rows, cache_len), 1).astype(F32) < length
    peak = jnp.maximum(
        jnp.max(jnp.where(valid, scores, -1e30), axis=1, keepdims=True), self_score
    )
    terms = jnp.where(valid, jnp.exp(scores - peak), 0.0)
    self_exp = jnp.exp(self_score - peak)
    total = jnp.sum(terms, axis=1, keepdims=True) + self_exp
    weights = (terms / total).reshape(rows, 8, cache_len).astype(BF16)
    self_weight = (self_exp / total).astype(BF16).astype(F32)
    ready("v_cache")
    mixed = jnp.einsum("bql,bld->bqd", weights, v_ref[...], preferred_element_type=F32)
    mixed = (mixed.reshape(8 * rows, lanes) + self_weight * value_self).astype(BF16)
    tall = (6 * rows, 8 * rows)
    i, j = iota(tall, 0), iota(tall, 1)
    gather = one_hot(((j >> 3) == (i & (rows - 1))) & ((j & 7) == (i >> log_rows)))
    out = dot(gather, mixed)
    head = [out[h * rows : (h + 1) * rows] for h in range(6)]
    return jnp.concatenate(
        [
            jnp.where(low, head[0], pltpu.roll(head[1], HEAD_DIM, 1)),
            jnp.where(low, head[2], head[3]),
            jnp.where(low, pltpu.roll(head[4], HEAD_DIM, 1), head[5]),
        ],
        axis=1,
    ).astype(BF16)


INPUTS = [
    "resid", "queries", "new_keys", "new_values", "k_cache", "v_cache", "lens", "w_out", "gain",
    "router", "routes", "gate", "up", "down",
]
HELD = [name for name in INPUTS if name not in ("gain", "router", "gate", "up", "down")]
LOADS = [
    "queries", "lens", "new_keys", "new_values", "k_cache", "gate", "up", "down", "v_cache",
    "w_out", "gain", "routes", "resid", "router",
]


def group_of(chips, ny):
    return min(chips, PLANES * ny)


def plan(nz, ny, nx, rows, width, units, shapes):
    vmem, dma = pltpu.VMEM, pltpu.SemaphoreType.DMA
    chips, experts, block = nz * ny, 2 * nz, CAP
    near = min(2, nx - 1)
    out = {name + "_v": vmem(shapes[name].shape, shapes[name].dtype) for name in HELD}
    out.update(
        part_own=vmem((nx, rows, width), F32),
        part_send=vmem((nx, rows, width), BF16),
        part_recv=vmem((nx - 1, rows, width), BF16),
        gathered=vmem((nx, rows, width), BF16),
        gain_all=vmem((nx,) + shapes["gain"].shape, F32),
        router_all=vmem((nx, experts, width), F32),
        gate_up=vmem((nx, 2, 2, width, units), BF16),
        down_all=vmem((nx, 2, units, width), BF16),
        rows_send=vmem((experts, block, width), BF16),
        rows_recv=vmem((chips, block, width), BF16),
        back_send=vmem((chips, block, width), BF16),
        back_recv=vmem((chips, block, width), BF16),
        moe_own=vmem((nx, rows, width), F32),
        moe_send=vmem((nx, rows, width), BF16),
        moe_recv=vmem((nx - 1, rows, width), BF16),
        load_sem=dma((len(INPUTS),)),
        one_sem=pltpu.SemaphoreType.REGULAR,
        two_sem=pltpu.SemaphoreType.REGULAR,
        line_sem=pltpu.SemaphoreType.REGULAR,
        gain_ss=dma((nx - 1,)),
        gain_rs=dma((nx - 1,)),
        router_ss=dma((nx - 1,)),
        router_rs=dma((nx - 1,)),
        part_ss=dma((nx - 1,)),
        part_rs=dma((nx - 1,)),
        gath_ss=dma((nx - 1,)),
        gath_rs=dma((nx - 1,)),
        near_ss=dma((near, 3)),
        near_rs=dma((near, 3)),
        far_ss=dma((4,)),
        far_rs=dma((4,)),
        core_ss=dma((nx, 3)),
        core_rs=dma((nx, 3)),
        disp_ss=dma(()),
        disp_rs=dma((chips // group_of(chips, ny),)),
        back_ss=dma(()),
        back_rs=dma(()),
        moe_ss=dma((nx - 1,)),
        moe_rs=dma((nx - 1,)),
    )
    return out


class Refs:
    pass


def kernel(nz, ny, nx, names, *args):
    r = Refs()
    for name, ref in zip(names, args):
        setattr(r, name, ref)
    rows, width = r.resid.shape
    depth = nx * width
    quad = ny // 2
    experts = 2 * nz
    chips = nz * ny
    per = CAP // nx
    units = r.gate.shape[1]
    req = lax.axis_index("req")
    x = lax.axis_index("tp")
    core = lax.rem(req, 2)
    chip = req // 2
    y = lax.rem(chip, ny)
    z = chip // ny
    here = z * ny + y
    partner = (req + 1 - 2 * core, x)

    def peer_x(step):
        return lax.rem(x + step, nx)

    def device_of(zz, yy):
        return ((zz * ny + yy) * 2 + core, x)

    def far_first(size):
        return sorted(range(size), key=lambda d: (-min(d, size - d), d))

    def far_apart():
        def key(offset):
            hops = [min(d, n - d) for d, n in zip(offset, (nz, ny))]
            return -sum(hops), hops[0], sum(d > n // 2 for d, n in zip(offset, (nz, ny))) % 2, offset

        return sorted(((a, b) for a in range(nz) for b in range(ny) if a or b), key=key)

    def remote(src, dst, ss, rs, device):
        return pltpu.make_async_remote_copy(
            src_ref=src, dst_ref=dst, send_sem=ss, recv_sem=rs, device_id=device,
            device_id_type=MESH,
        )

    def gate_at(xs):
        return r.gate_up.at[xs, core, 0]

    def up_at(xs):
        return r.gate_up.at[xs, core, 1]

    def down_at(xs):
        return r.down_all.at[xs, core]

    places = (gate_at, up_at, down_at)

    targets = dict(
        gain=r.gain_all.at[x], router=r.router_all.at[x], gate=gate_at(x), up=up_at(x),
        down=down_at(x),
    )
    loads = {}
    for name in LOADS:
        target = targets[name] if name in targets else getattr(r, name + "_v")
        sem = r.load_sem.at[INPUTS.index(name)]
        loads[name] = pltpu.make_async_copy(getattr(r, name), target, sem)
        loads[name].start()

    def ready(name):
        loads[name].wait()

    barrier = pltpu.get_barrier_semaphore()

    def signal(sem, device):
        pl.semaphore_signal(sem, inc=1, device_id=device, device_id_type=MESH)

    def apart(d):
        along_y = {d % ny, -d % ny} - {0} if d < ny else set()
        along_z = {d % nz, -d % nz} - {0} if d < nz else set()
        return [device_of(z, lax.rem(y + k, ny)) for k in sorted(along_y)] + [
            device_of(lax.rem(z + k, nz), y) for k in sorted(along_z)
        ]

    line_z = [device_of(lax.rem(z + d, nz), y) for d in far_first(nz) if d]
    for step in range(1, nx):
        signal(barrier, (req, peer_x(step)))
    signal(barrier, partner)
    for device in apart(1):
        signal(barrier, device)

    near = (1, nx - 1) if nx > 2 else (1,)
    near_copies = {
        (n, k): remote(
            places[k](x), places[k](x), r.near_ss.at[n, k], r.near_rs.at[n, k],
            (req, peer_x(step)),
        )
        for k in range(3)
        for n, step in enumerate(near)
    }
    core_copies = []

    def core_send(step, k):
        ref = places[k](peer_x(step))
        copy = remote(ref, ref, r.core_ss.at[step, k], r.core_rs.at[step, k], partner)
        copy.start()
        core_copies.append(copy)

    def meanwhile():
        pl.semaphore_wait(barrier, nx + len(apart(1)))
        for device in apart(1):
            signal(r.one_sem, device)
        for k, name in enumerate(("gate", "up", "down")):
            ready(name)
            if k == 0:
                for n in range(len(near)):
                    near_copies[n, 0].start()
            core_send(0, k)

    attention = attend(
        r.queries_v, r.new_keys_v, r.new_values_v, r.k_cache_v, r.v_cache_v, r.lens_v, rows, ready,
        meanwhile,
    )
    ready("w_out")
    for f in range(nx):
        share = dot(attention, r.w_out_v[:, f * width : (f + 1) * width])
        r.part_own[f] = share
        r.part_send[f] = share.astype(BF16)

    ready("gain")
    part_copies, gain_copies = [], []
    for step in range(1, nx):
        n, to = step - 1, peer_x(step)
        part_copies.append(
            remote(r.part_send.at[to], r.part_recv.at[n], r.part_ss.at[n], r.part_rs.at[n], (req, to))
        )
        part_copies[n].start()
    for step in range(1, nx):
        n, to = step - 1, peer_x(step)
        gain_copies.append(
            remote(r.gain_all.at[x], r.gain_all.at[x], r.gain_ss.at[n], r.gain_rs.at[n], (req, to))
        )
        gain_copies[n].start()

    for n in range(len(near)):
        near_copies[n, 1].start()
    pl.semaphore_wait(r.one_sem, len(apart(1)))
    for device in apart(2):
        signal(r.two_sem, device)

    ready("routes")
    routes = r.routes_v[...]
    block = nx * per
    log_rows, log_per = shift_of(rows), shift_of(per)
    e_rows = iota((experts, rows), 0)
    names_e = one_hot((e_rows == routes[0:1, :]) | (e_rows == routes[1:2, :]), F32)
    before = one_hot(iota((rows, rows), 0) < iota((rows, rows), 1))
    rank = names_e * (dot(names_e.astype(BF16), before) + 1.0)
    tall = (experts * block, experts)
    lift = one_hot((iota(tall, 0) >> 3) == iota(tall, 1))
    flat = (rows, nx * rows)
    fan = one_hot(iota(flat, 0) == (iota(flat, 1) & (rows - 1)))
    value = dot(dot(lift, rank.astype(BF16)).astype(BF16), fan)
    full = (experts * block, nx * rows)
    i, j = iota(full, 0), iota(full, 1)
    wanted = (x * per + (i & (per - 1)) + 1).astype(F32)
    pick = one_hot((value == wanted) & (((i & 7) >> log_per) == (j >> log_rows)))

    eye = one_hot(iota((rows, rows), 0) == iota((rows, rows), 1))
    e_cols = iota((rows, experts), 1).astype(F32)

    def column(k):
        row = jnp.broadcast_to(routes[k : k + 1, :], (8, rows)).astype(F32).astype(BF16)
        return dot_nt(eye, row)[:, 0:1]

    first = one_hot(column(0) == e_cols, F32)
    second = one_hot(column(1) == e_cols, F32)
    earlier = one_hot(iota((rows, rows), 1) < iota((rows, rows), 0))
    count = dot(earlier, (first + second).astype(BF16)) + 1.0
    wide = (experts, experts * block)
    reach = one_hot(iota(wide, 0) == (iota(wide, 1) >> 3))
    slot = iota((rows, experts * block), 1)
    target = (x * per + (slot & (per - 1)) + 1).astype(F32)
    slot_f = (slot & 7) >> log_per
    collect = []
    for marks in (first, second):
        held = dot((marks * count).astype(BF16), reach) == target
        for f in range(nx):
            collect.append(one_hot(held & (slot_f == f), F32))
    collect = jnp.concatenate(collect, axis=0)

    group = group_of(chips, ny)
    batch = group * block
    log_f = shift_of(group * per)
    i, j = iota((batch, batch), 0), iota((batch, batch), 1)

    def same_row(a, b):
        return one_hot(
            ((a >> log_f) == ((b & 7) >> log_per))
            & (((a & (group * per - 1)) >> log_per) == (b >> 3))
            & ((a & (per - 1)) == (b & (per - 1)))
        )

    order_in, order_out = same_row(i, j), same_row(j, i)

    if apart(2):
        pl.semaphore_wait(r.two_sem, len(apart(2)))
    for device in line_z:
        signal(r.line_sem, device)

    ready("resid")
    for copy in part_copies:
        copy.wait_recv()
    summed = r.resid_v[...].astype(F32) + r.part_own[x]
    for n in range(nx - 1):
        summed = summed + r.part_recv[n].astype(F32)
    attended = summed.astype(BF16)
    r.gathered[x] = attended
    gath_copies = []
    for step in range(1, nx):
        n, to = step - 1, peer_x(step)
        gath_copies.append(
            remote(r.gathered.at[x], r.gathered.at[x], r.gath_ss.at[n], r.gath_rs.at[n], (req, to))
        )
        gath_copies[n].start()
    for n in range(len(near)):
        near_copies[n, 2].start()
    for n in range(len(near)):
        near_copies[n, 0].wait_recv()
    for step in near:
        core_send(step, 0)
    left, right = peer_x(nx - 1), peer_x(1)
    far_copies = []

    def pass_far(ref, to):
        n = len(far_copies)
        far_copies.append(remote(ref, ref, r.far_ss.at[n], r.far_rs.at[n], (req, to)))
        far_copies[n].start()

    r.att_out[...] = attended
    if nz > 1:
        pl.semaphore_wait(r.line_sem, nz - 1)
    for copy in gain_copies:
        copy.wait_recv()
    gains = [
        jnp.concatenate([r.gain_all[f, k : k + 1, :] for k in range(width // 128)], axis=1)
        for f in range(nx)
    ]

    for copy in gath_copies:
        copy.wait_recv()
    for n in range(len(near)):
        near_copies[n, 1].wait_recv()
    if nx > 2:
        pass_far(gate_at(left), right)
        pass_far(up_at(right), left)
    for step in near:
        core_send(step, 1)

    att = [r.gathered[f].astype(F32) for f in range(nx)]
    square = jnp.sum(att[0] * att[0], axis=1, keepdims=True)
    for f in range(1, nx):
        square = square + jnp.sum(att[f] * att[f], axis=1, keepdims=True)
    inv_rms = 1.0 / jnp.sqrt(square / depth + 1e-06)
    scaled = [att[f] * gains[f] for f in range(nx)]
    normed = jnp.concatenate([(scaled[f] * inv_rms).astype(BF16) for f in range(nx)], axis=0)
    r.rows_send[...] = dot(pick, normed).reshape(experts, block, width).astype(BF16)

    plane = z // (group // ny)
    for dz, dy in far_apart():
        zz, yy = lax.rem(z + dz, nz), lax.rem(y + dy, ny)
        remote(
            r.rows_send.at[2 * zz + yy // quad], r.rows_recv.at[here], r.disp_ss,
            r.disp_rs.at[plane], device_of(zz, yy),
        ).start()
    keep = pltpu.make_async_copy(
        r.rows_send.at[2 * z + y // quad], r.rows_recv.at[here], r.disp_rs.at[plane]
    )
    keep.start()

    half = units // 2
    for n in range(len(near)):
        near_copies[n, 2].wait_recv()
    if nx > 2:
        pass_far(r.down_all.at[left, core, pl.ds(0, half)], right)
        pass_far(r.down_all.at[right, core, pl.ds(half, half)], left)
    for step in near:
        core_send(step, 2)
    ready("router")
    router_copies = []
    for step in range(1, nx):
        n, to = step - 1, peer_x(step)
        router_copies.append(
            remote(r.router_all.at[x], r.router_all.at[x], r.router_ss.at[n], r.router_rs.at[n], (req, to))
        )
        router_copies[n].start()
    if nx > 2:
        for k, copies in enumerate((far_copies[:1], far_copies[1:2], far_copies[2:])):
            for copy in copies:
                copy.wait_recv()
            core_send(2, k)

    groups = chips // group
    halves = [range(groups)] if groups < 2 else [range(groups // 2), range(groups // 2, groups)]
    lot = group * per

    def expert(lhs):
        both = None
        for f in range(nx):
            rhs = jnp.concatenate([r.gate_up[f, c, k] for k in range(2) for c in range(2)], axis=1)
            both = dot(lhs[f], rhs) if f == 0 else both + dot(lhs[f], rhs)
        gate, up = both[:, : 2 * units], both[:, 2 * units :]
        hidden = (gate / (1.0 + jnp.exp(-gate)) * up).astype(BF16)
        return [
            dot(hidden, jnp.concatenate([r.down_all[f, c] for c in range(2)], axis=0)).astype(BF16)
            for f in range(nx)
        ]

    for turn, half in enumerate(halves):
        arrived = []
        for g in half:
            part = r.rows_recv.at[pl.ds(g * group, group)]
            remote(part, part, r.disp_ss, r.disp_rs.at[g], (req, x)).wait_recv()
            arrived.append(dot(order_in, part[...].reshape(batch, width)).astype(BF16))
        if turn == 0:
            for copy in core_copies:
                copy.wait_recv()
        outs = expert(
            [
                jnp.concatenate([a[f * lot : (f + 1) * lot] for a in arrived], axis=0)
                for f in range(nx)
            ]
        )
        for k, g in enumerate(half):
            stack = jnp.concatenate([out[k * lot : (k + 1) * lot] for out in outs], axis=0)
            r.back_send[g * group : (g + 1) * group] = (
                dot(order_out, stack).reshape(group, block, width).astype(BF16)
            )
            for zz in range(g * (group // ny), (g + 1) * (group // ny)):
                for dy in far_first(ny):
                    yy = lax.rem(y + dy, ny)

                    def send():
                        remote(
                            r.back_send.at[zz * ny + yy], r.back_recv.at[here], r.back_ss,
                            r.back_rs, device_of(zz, yy),
                        ).start()

                    if dy:
                        send()
                    else:
                        pl.when(zz != z)(send)
    keep_back = pltpu.make_async_copy(r.back_send.at[here], r.back_recv.at[here], r.back_rs)
    keep_back.start()

    for copy in router_copies:
        copy.wait_recv()
    logits = dot_nt(scaled[0], r.router_all[0], HIGHEST)
    for f in range(1, nx):
        logits = logits + dot_nt(scaled[f], r.router_all[f], HIGHEST)
    logits = logits * inv_rms
    gap = jnp.sum(logits * first, axis=1, keepdims=True) - jnp.sum(
        logits * second, axis=1, keepdims=True
    )
    first_weight = jax.nn.sigmoid(gap)
    second_weight = 1.0 - first_weight

    remote(r.back_recv, r.back_recv, r.back_ss, r.back_rs, (req, x)).wait_recv()
    came = r.back_recv[...].astype(F32).reshape(experts, quad, block, width)
    out_rows = came[:, 0]
    for k in range(1, quad):
        out_rows = out_rows + came[:, k]
    split = dot(collect, out_rows.reshape(experts * block, width), HIGHEST)
    for f in range(nx):
        moe = (
            first_weight * split[f * rows : (f + 1) * rows]
            + second_weight * split[(nx + f) * rows : (nx + f + 1) * rows]
        )
        r.moe_own[f] = moe
        r.moe_send[f] = moe.astype(BF16)
    moe_copies = []
    for step in range(1, nx):
        n, to = step - 1, peer_x(step)
        moe_copies.append(
            remote(r.moe_send.at[to], r.moe_recv.at[n], r.moe_ss.at[n], r.moe_rs.at[n], (req, to))
        )
        moe_copies[n].start()

    for copy in part_copies + gain_copies + gath_copies + router_copies:
        copy.wait_send()
    for copy in list(near_copies.values()) + far_copies + core_copies:
        copy.wait_send()
    rest = r.rows_recv.at[pl.ds(0, chips - 1)]
    remote(rest, rest, r.disp_ss, r.disp_rs, (req, x)).wait_send()
    rest = r.back_recv.at[pl.ds(0, chips - 1)]
    remote(rest, rest, r.back_ss, r.back_rs, (req, x)).wait_send()

    for copy in moe_copies:
        copy.wait_recv()
    moe = r.moe_own[x]
    for n in range(nx - 1):
        moe = moe + r.moe_recv[n].astype(F32)
    r.layer_out[...] = (attended.astype(F32) + moe).astype(BF16)
    for copy in moe_copies:
        copy.wait_send()


def pass_on(a_in, b_in, a_out, b_out):
    a_out[...] = a_in[...]
    b_out[...] = b_in[...]


def shards(nz, ny, nx, resid, queries, new_keys, new_values, k_cache, v_cache, lengths, w_out,
           norm_gain, w_router, routes, w_gate, w_up, w_down):
    rows, width = resid.shape
    units = w_gate.shape[2]
    operands = (
        resid, queries, new_keys, new_values, k_cache, v_cache, lengths.reshape(1, rows), w_out,
        norm_gain.reshape(width // 128, 128), w_router.T, routes.T, w_gate[0], w_up[0], w_down[0],
    )
    scratch = plan(nz, ny, nx, rows, width, units, dict(zip(INPUTS, operands)))
    names = INPUTS + ["att_out", "layer_out"] + list(scratch)
    out = jax.ShapeDtypeStruct((rows, width), BF16)
    whole = pl.BlockSpec(memory_space=pltpu.VMEM)
    results = pl.pallas_call(
        functools.partial(kernel, nz, ny, nx, names),
        out_shape=(pltpu.VMEM((rows, width), BF16),) * 2,
        in_specs=[pl.BlockSpec(memory_space=pl.ANY)] * len(operands),
        out_specs=[whole] * 2,
        scratch_shapes=list(scratch.values()),
        compiler_params=pltpu.CompilerParams(
            collective_id=0, has_side_effects=True, vmem_limit_bytes=56 * 1024 * 1024
        ),
    )(*operands)
    return pl.pallas_call(
        pass_on, out_shape=(out, out), in_specs=[whole] * 2, out_specs=[whole] * 2
    )(*(pltpu.with_memory_space_constraint(a, pltpu.VMEM) for a in results))


def solution(mesh):
    nx = mesh.shape["tp"]
    nz = NZ
    ny = mesh.shape["req"] // (2 * nz)
    placed = (
        P("req", "tp"),
        P("req", "tp"),
        P("req", "tp"),
        P("req", "tp"),
        P("req", None, "tp"),
        P("req", None, "tp"),
        P("req"),
        P("tp", None),
        P("tp"),
        P("tp", None),
        P("req", None),
        P("req", "tp", None),
        P("req", "tp", None),
        P("req", None, "tp"),
    )
    return jax.shard_map(
        functools.partial(shards, nz, ny, nx),
        mesh=mesh,
        in_specs=placed,
        out_specs=(P("req", "tp"), P("req", "tp")),
        check_vma=False,
    )
```

```python
import functools
import math

import jax
import jax.numpy as jnp
from jax import lax
from jax.experimental import pallas as pl
from jax.experimental.pallas import tpu as pltpu
from jax.sharding import PartitionSpec as P

HEAD_DIM = 64
CAP = 8
NZ = 8
NY = 8
PLANES = 2
MESH = pl.DeviceIdType.MESH
HIGHEST = lax.Precision.HIGHEST
F32 = jnp.float32
BF16 = jnp.bfloat16


def iota(shape, axis):
    return lax.broadcasted_iota(jnp.int32, shape, axis)


def shift_of(n):
    return int(math.log2(n))


def one_hot(mask, dtype=BF16):
    return jnp.where(mask, 1.0, 0.0).astype(dtype)


def dot(a, b, precision=None):
    return jnp.dot(a, b, preferred_element_type=F32, precision=precision)


def dot_nt(a, b, precision=None):
    return lax.dot_general(
        a, b, (((1,), (1,)), ((), ())), preferred_element_type=F32, precision=precision
    )


def attend(queries_ref, new_keys_ref, new_values_ref, k_ref, v_ref, lens_ref, rows, ready, meanwhile):
    lanes = 2 * HEAD_DIM
    ready("queries")
    queries = queries_ref[...]
    low = iota((rows, lanes), 1) < HEAD_DIM
    chunks = [queries[:, i * lanes : (i + 1) * lanes].astype(F32) for i in range(3)]
    turned = [pltpu.roll(chunks[0], HEAD_DIM, 1), None, pltpu.roll(chunks[2], HEAD_DIM, 1)]
    zero = jnp.zeros((rows, lanes), F32)
    heads = jnp.concatenate(
        [
            jnp.where(low, chunks[0], zero),
            jnp.where(low, turned[0], zero),
            jnp.where(low, chunks[1], zero),
            jnp.where(low, zero, chunks[1]),
            jnp.where(low, zero, turned[2]),
            jnp.where(low, zero, chunks[2]),
        ],
        axis=0,
    ).astype(BF16)
    log_rows = shift_of(rows)
    wide = (8 * rows, 6 * rows)
    i, j = iota(wide, 0), iota(wide, 1)
    spread = one_hot(((i >> 3) == (j & (rows - 1))) & ((i & 7) == (j >> log_rows)))
    query = dot(spread, heads)
    narrow = (8 * rows, rows)
    owner = one_hot((iota(narrow, 0) >> 3) == iota(narrow, 1))
    ready("lens")
    lens = lens_ref[...]
    length = dot_nt(owner, jnp.broadcast_to(lens.astype(F32), (8, rows)).astype(BF16))[:, 0:1]
    ready("new_keys")
    ready("new_values")
    key_self = dot(owner, new_keys_ref[...])
    value_self = dot(owner, new_values_ref[...])
    scale = 1.0 / math.sqrt(HEAD_DIM)
    cache_len = k_ref.shape[1]
    meanwhile()
    ready("k_cache")
    query3 = query.reshape(rows, 8, lanes).astype(BF16)
    scores = (
        jnp.einsum("bqd,bld->bql", query3, k_ref[...], preferred_element_type=F32) * scale
    ).reshape(8 * rows, cache_len)
    self_score = jnp.sum(query * key_self, axis=1, keepdims=True) * scale
    valid = iota((8 * rows, cache_len), 1).astype(F32) < length
    peak = jnp.maximum(
        jnp.max(jnp.where(valid, scores, -1e30), axis=1, keepdims=True), self_score
    )
    terms = jnp.where(valid, jnp.exp(scores - peak), 0.0)
    self_exp = jnp.exp(self_score - peak)
    total = jnp.sum(terms, axis=1, keepdims=True) + self_exp
    weights = (terms / total).reshape(rows, 8, cache_len).astype(BF16)
    self_weight = (self_exp / total).astype(BF16).astype(F32)
    ready("v_cache")
    mixed = jnp.einsum("bql,bld->bqd", weights, v_ref[...], preferred_element_type=F32)
    mixed = (mixed.reshape(8 * rows, lanes) + self_weight * value_self).astype(BF16)
    tall = (6 * rows, 8 * rows)
    i, j = iota(tall, 0), iota(tall, 1)
    gather = one_hot(((j >> 3) == (i & (rows - 1))) & ((j & 7) == (i >> log_rows)))
    out = dot(gather, mixed)
    head = [out[h * rows : (h + 1) * rows] for h in range(6)]
    return jnp.concatenate(
        [
            jnp.where(low, head[0], pltpu.roll(head[1], HEAD_DIM, 1)),
            jnp.where(low, head[2], head[3]),
            jnp.where(low, pltpu.roll(head[4], HEAD_DIM, 1), head[5]),
        ],
        axis=1,
    ).astype(BF16)


INPUTS = [
    "resid", "queries", "new_keys", "new_values", "k_cache", "v_cache", "lens", "w_out", "gain",
    "router", "routes", "gate", "up", "down",
]
HELD = [name for name in INPUTS if name not in ("gain", "router", "gate", "up", "down")]
LOADS = [
    "queries", "lens", "new_keys", "new_values", "k_cache", "gate", "up", "down", "v_cache",
    "w_out", "gain", "routes", "resid", "router",
]


def group_of(chips, ny):
    return min(chips, PLANES * ny)


def plan(nz, ny, nx, rows, width, units, shapes):
    vmem, dma = pltpu.VMEM, pltpu.SemaphoreType.DMA
    chips, experts, block = nz * ny, 2 * nz, CAP
    near = min(2, nx - 1)
    out = {name + "_v": vmem(shapes[name].shape, shapes[name].dtype) for name in HELD}
    out.update(
        part_send=vmem((nx - 1, rows, width), BF16),
        part_recv=vmem((nx - 1, rows, width), BF16),
        gathered=vmem((nx, rows, width), BF16),
        gain_all=vmem((nx,) + shapes["gain"].shape, F32),
        router_all=vmem((nx, experts, width), F32),
        gate_up=vmem((nx, 2, 2, width, units), BF16),
        down_all=vmem((nx, 2, units, width), BF16),
        rows_send=vmem((experts, block, width), BF16),
        rows_recv=vmem((chips, block, width), BF16),
        back_send=vmem((chips, block, width), BF16),
        back_recv=vmem((chips, block, width), BF16),
        moe_own=vmem((nx, rows, width), F32),
        moe_send=vmem((nx, rows, width), BF16),
        moe_recv=vmem((nx - 1, rows, width), BF16),
        load_sem=dma((len(INPUTS),)),
        one_sem=pltpu.SemaphoreType.REGULAR,
        two_sem=pltpu.SemaphoreType.REGULAR,
        line_sem=pltpu.SemaphoreType.REGULAR,
        gain_ss=dma((nx - 1,)),
        gain_rs=dma((nx - 1,)),
        router_ss=dma((nx - 1,)),
        router_rs=dma((nx - 1,)),
        part_ss=dma((nx - 1,)),
        part_rs=dma((nx - 1,)),
        gath_ss=dma((nx - 1,)),
        gath_rs=dma((nx - 1,)),
        near_ss=dma((near, 3)),
        near_rs=dma((near, 3)),
        far_ss=dma((4,)),
        far_rs=dma((4,)),
        core_ss=dma((nx, 3)),
        core_rs=dma((nx, 3)),
        disp_ss=dma(()),
        disp_rs=dma((chips // group_of(chips, ny),)),
        back_ss=dma(()),
        back_rs=dma(()),
        moe_ss=dma((nx - 1,)),
        moe_rs=dma((nx - 1,)),
    )
    return out


class Refs:
    pass


def kernel(nz, ny, nx, names, *args):
    r = Refs()
    for name, ref in zip(names, args):
        setattr(r, name, ref)
    rows, width = r.resid.shape
    depth = nx * width
    quad = ny // 2
    experts = 2 * nz
    chips = nz * ny
    per = CAP // nx
    units = r.gate.shape[1]
    req = lax.axis_index("req")
    x = lax.axis_index("tp")
    core = lax.rem(req, 2)
    chip = req // 2
    y = lax.rem(chip, ny)
    z = chip // ny
    here = z * ny + y
    partner = (req + 1 - 2 * core, x)

    def peer_x(step):
        return lax.rem(x + step, nx)

    def device_of(zz, yy):
        return ((zz * ny + yy) * 2 + core, x)

    def far_first(size):
        return sorted(range(size), key=lambda d: (-min(d, size - d), d))

    def far_apart():
        def key(offset):
            hops = [min(d, n - d) for d, n in zip(offset, (nz, ny))]
            return -sum(hops), hops[0], sum(d > n // 2 for d, n in zip(offset, (nz, ny))) % 2, offset

        return sorted(((a, b) for a in range(nz) for b in range(ny) if a or b), key=key)

    def remote(src, dst, ss, rs, device):
        return pltpu.make_async_remote_copy(
            src_ref=src, dst_ref=dst, send_sem=ss, recv_sem=rs, device_id=device,
            device_id_type=MESH,
        )

    def gate_at(xs):
        return r.gate_up.at[xs, core, 0]

    def up_at(xs):
        return r.gate_up.at[xs, core, 1]

    def down_at(xs):
        return r.down_all.at[xs, core]

    places = (gate_at, up_at, down_at)

    targets = dict(
        gain=r.gain_all.at[x], router=r.router_all.at[x], gate=gate_at(x), up=up_at(x),
        down=down_at(x),
    )
    loads = {}
    for name in LOADS:
        target = targets[name] if name in targets else getattr(r, name + "_v")
        sem = r.load_sem.at[INPUTS.index(name)]
        loads[name] = pltpu.make_async_copy(getattr(r, name), target, sem)
        loads[name].start()

    def ready(name):
        loads[name].wait()

    barrier = pltpu.get_barrier_semaphore()

    def signal(sem, device):
        pl.semaphore_signal(sem, inc=1, device_id=device, device_id_type=MESH)

    def apart(d):
        along_y = {d % ny, -d % ny} - {0} if d < ny else set()
        along_z = {d % nz, -d % nz} - {0} if d < nz else set()
        return [device_of(z, lax.rem(y + k, ny)) for k in sorted(along_y)] + [
            device_of(lax.rem(z + k, nz), y) for k in sorted(along_z)
        ]

    line_z = [device_of(lax.rem(z + d, nz), y) for d in far_first(nz) if d]
    for step in range(1, nx):
        signal(barrier, (req, peer_x(step)))
    signal(barrier, partner)
    for device in apart(1):
        signal(barrier, device)

    near = (1, nx - 1) if nx > 2 else (1,)
    near_copies = {
        (n, k): remote(
            places[k](x), places[k](x), r.near_ss.at[n, k], r.near_rs.at[n, k],
            (req, peer_x(step)),
        )
        for k in range(3)
        for n, step in enumerate(near)
    }
    core_copies = []

    def core_send(step, k):
        ref = places[k](peer_x(step))
        copy = remote(ref, ref, r.core_ss.at[step, k], r.core_rs.at[step, k], partner)
        copy.start()
        core_copies.append(copy)

    def meanwhile():
        pl.semaphore_wait(barrier, nx + len(apart(1)))
        for device in apart(1):
            signal(r.one_sem, device)
        for k, name in enumerate(("gate", "up", "down")):
            ready(name)
            if k == 0:
                for n in range(len(near)):
                    near_copies[n, 0].start()
            core_send(0, k)

    attention = attend(
        r.queries_v, r.new_keys_v, r.new_values_v, r.k_cache_v, r.v_cache_v, r.lens_v, rows, ready,
        meanwhile,
    )
    ready("w_out")

    def project(f):
        return dot(attention, r.w_out_v[:, pl.ds(pl.multiple_of(f * width, width), width)])

    others = sorted(range(1, nx), key=lambda d: (-min(d, nx - d), d))
    part_copies, gain_copies = [], []
    for n, step in enumerate(others):
        to = peer_x(step)
        r.part_send[n] = project(to).astype(BF16)
        part_copies.append(
            remote(r.part_send.at[n], r.part_recv.at[n], r.part_ss.at[n], r.part_rs.at[n], (req, to))
        )
        part_copies[n].start()
    part_own = project(x)
    ready("gain")
    for n, step in enumerate(others):
        to = peer_x(step)
        gain_copies.append(
            remote(r.gain_all.at[x], r.gain_all.at[x], r.gain_ss.at[n], r.gain_rs.at[n], (req, to))
        )
        gain_copies[n].start()

    for n in range(len(near)):
        near_copies[n, 1].start()
    pl.semaphore_wait(r.one_sem, len(apart(1)))
    for device in apart(2):
        signal(r.two_sem, device)

    ready("routes")
    routes = r.routes_v[...]
    block = nx * per
    log_rows, log_per = shift_of(rows), shift_of(per)
    e_rows = iota((experts, rows), 0)
    names_e = one_hot((e_rows == routes[0:1, :]) | (e_rows == routes[1:2, :]), F32)
    before = one_hot(iota((rows, rows), 0) < iota((rows, rows), 1))
    rank = names_e * (dot(names_e.astype(BF16), before) + 1.0)
    tall = (experts * block, experts)
    lift = one_hot((iota(tall, 0) >> 3) == iota(tall, 1))
    flat = (rows, nx * rows)
    fan = one_hot(iota(flat, 0) == (iota(flat, 1) & (rows - 1)))
    value = dot(dot(lift, rank.astype(BF16)).astype(BF16), fan)
    full = (experts * block, nx * rows)
    i, j = iota(full, 0), iota(full, 1)
    wanted = (x * per + (i & (per - 1)) + 1).astype(F32)
    pick = one_hot((value == wanted) & (((i & 7) >> log_per) == (j >> log_rows)))

    eye = one_hot(iota((rows, rows), 0) == iota((rows, rows), 1))
    e_cols = iota((rows, experts), 1).astype(F32)

    def column(k):
        row = jnp.broadcast_to(routes[k : k + 1, :], (8, rows)).astype(F32).astype(BF16)
        return dot_nt(eye, row)[:, 0:1]

    first = one_hot(column(0) == e_cols, F32)
    second = one_hot(column(1) == e_cols, F32)
    earlier = one_hot(iota((rows, rows), 1) < iota((rows, rows), 0))
    count = dot(earlier, (first + second).astype(BF16)) + 1.0
    wide = (experts, experts * block)
    reach = one_hot(iota(wide, 0) == (iota(wide, 1) >> 3))
    slot = iota((rows, experts * block), 1)
    target = (x * per + (slot & (per - 1)) + 1).astype(F32)
    slot_f = (slot & 7) >> log_per
    collect = []
    for marks in (first, second):
        held = dot((marks * count).astype(BF16), reach) == target
        for f in range(nx):
            collect.append(one_hot(held & (slot_f == f), F32))
    collect = jnp.concatenate(collect, axis=0)

    group = group_of(chips, ny)
    batch = group * block
    log_f = shift_of(group * per)
    i, j = iota((batch, batch), 0), iota((batch, batch), 1)

    def same_row(a, b):
        return one_hot(
            ((a >> log_f) == ((b & 7) >> log_per))
            & (((a & (group * per - 1)) >> log_per) == (b >> 3))
            & ((a & (per - 1)) == (b & (per - 1)))
        )

    order_in, order_out = same_row(i, j), same_row(j, i)

    if apart(2):
        pl.semaphore_wait(r.two_sem, len(apart(2)))
    for device in line_z:
        signal(r.line_sem, device)

    ready("resid")
    for copy in part_copies:
        copy.wait_recv()
    summed = r.resid_v[...].astype(F32) + part_own
    for n in range(nx - 1):
        summed = summed + r.part_recv[n].astype(F32)
    attended = summed.astype(BF16)
    r.gathered[x] = attended
    gath_copies = []
    for n, step in enumerate(others):
        to = peer_x(step)
        gath_copies.append(
            remote(r.gathered.at[x], r.gathered.at[x], r.gath_ss.at[n], r.gath_rs.at[n], (req, to))
        )
        gath_copies[n].start()
    for n in range(len(near)):
        near_copies[n, 2].start()
    for n in range(len(near)):
        near_copies[n, 0].wait_recv()
    for step in near:
        core_send(step, 0)
    left, right = peer_x(nx - 1), peer_x(1)
    far_copies = []

    def pass_far(ref, to):
        n = len(far_copies)
        far_copies.append(remote(ref, ref, r.far_ss.at[n], r.far_rs.at[n], (req, to)))
        far_copies[n].start()

    for n in range(len(near)):
        near_copies[n, 1].wait_recv()
    if nx > 2:
        pass_far(gate_at(left), right)
        pass_far(up_at(right), left)
    for step in near:
        core_send(step, 1)
    r.att_out[...] = attended
    if nz > 1:
        pl.semaphore_wait(r.line_sem, nz - 1)
    for copy in gain_copies:
        copy.wait_recv()
    gains = [
        jnp.concatenate([r.gain_all[f, k : k + 1, :] for k in range(width // 128)], axis=1)
        for f in range(nx)
    ]

    for copy in gath_copies:
        copy.wait_recv()

    att = [r.gathered[f].astype(F32) for f in range(nx)]
    square = jnp.sum(att[0] * att[0], axis=1, keepdims=True)
    for f in range(1, nx):
        square = square + jnp.sum(att[f] * att[f], axis=1, keepdims=True)
    inv_rms = 1.0 / jnp.sqrt(square / depth + 1e-06)
    scaled = [att[f] * gains[f] for f in range(nx)]
    normed = jnp.concatenate([(scaled[f] * inv_rms).astype(BF16) for f in range(nx)], axis=0)
    r.rows_send[...] = dot(pick, normed).reshape(experts, block, width).astype(BF16)

    plane = z // (group // ny)
    for dz, dy in far_apart():
        zz, yy = lax.rem(z + dz, nz), lax.rem(y + dy, ny)
        remote(
            r.rows_send.at[2 * zz + yy // quad], r.rows_recv.at[here], r.disp_ss,
            r.disp_rs.at[plane], device_of(zz, yy),
        ).start()
    keep = pltpu.make_async_copy(
        r.rows_send.at[2 * z + y // quad], r.rows_recv.at[here], r.disp_rs.at[plane]
    )
    keep.start()

    half = units // 2
    for n in range(len(near)):
        near_copies[n, 2].wait_recv()
    if nx > 2:
        pass_far(r.down_all.at[left, core, pl.ds(0, half)], right)
        pass_far(r.down_all.at[right, core, pl.ds(half, half)], left)
    for step in near:
        core_send(step, 2)
    ready("router")
    router_copies = []
    for n, step in enumerate(others):
        to = peer_x(step)
        router_copies.append(
            remote(r.router_all.at[x], r.router_all.at[x], r.router_ss.at[n], r.router_rs.at[n], (req, to))
        )
        router_copies[n].start()
    if nx > 2:
        for k, copies in enumerate((far_copies[:1], far_copies[1:2], far_copies[2:])):
            for copy in copies:
                copy.wait_recv()
            core_send(2, k)

    groups = chips // group
    cuts = sorted({0, groups // 4, groups // 2, groups})
    halves = [range(a, b) for a, b in zip(cuts, cuts[1:])]
    lot = group * per

    def expert(lhs):
        both = None
        for f in range(nx):
            rhs = jnp.concatenate([r.gate_up[f, c, k] for k in range(2) for c in range(2)], axis=1)
            both = dot(lhs[f], rhs) if f == 0 else both + dot(lhs[f], rhs)
        gate, up = both[:, : 2 * units], both[:, 2 * units :]
        hidden = (gate / (1.0 + jnp.exp(-gate)) * up).astype(BF16)
        return [
            dot(hidden, jnp.concatenate([r.down_all[f, c] for c in range(2)], axis=0)).astype(BF16)
            for f in range(nx)
        ]

    for turn, half in enumerate(halves):
        arrived = []
        for g in half:
            part = r.rows_recv.at[pl.ds(g * group, group)]
            remote(part, part, r.disp_ss, r.disp_rs.at[g], (req, x)).wait_recv()
            arrived.append(dot(order_in, part[...].reshape(batch, width)).astype(BF16))
        if turn == 0:
            for copy in core_copies:
                copy.wait_recv()
        outs = expert(
            [
                jnp.concatenate([a[f * lot : (f + 1) * lot] for a in arrived], axis=0)
                for f in range(nx)
            ]
        )
        for k, g in enumerate(half):
            stack = jnp.concatenate([out[k * lot : (k + 1) * lot] for out in outs], axis=0)
            r.back_send[g * group : (g + 1) * group] = (
                dot(order_out, stack).reshape(group, block, width).astype(BF16)
            )
            for zz in range(g * (group // ny), (g + 1) * (group // ny)):
                for dy in far_first(ny):
                    yy = lax.rem(y + dy, ny)

                    def send():
                        remote(
                            r.back_send.at[zz * ny + yy], r.back_recv.at[here], r.back_ss,
                            r.back_rs, device_of(zz, yy),
                        ).start()

                    if dy:
                        send()
                    else:
                        pl.when(zz != z)(send)
    keep_back = pltpu.make_async_copy(r.back_send.at[here], r.back_recv.at[here], r.back_rs)
    keep_back.start()

    for copy in router_copies:
        copy.wait_recv()
    logits = dot_nt(scaled[0], r.router_all[0], HIGHEST)
    for f in range(1, nx):
        logits = logits + dot_nt(scaled[f], r.router_all[f], HIGHEST)
    logits = logits * inv_rms
    gap = jnp.sum(logits * first, axis=1, keepdims=True) - jnp.sum(
        logits * second, axis=1, keepdims=True
    )
    first_weight = jax.nn.sigmoid(gap)
    second_weight = 1.0 - first_weight

    remote(r.back_recv, r.back_recv, r.back_ss, r.back_rs, (req, x)).wait_recv()
    came = r.back_recv[...].astype(F32).reshape(experts, quad, block, width)
    out_rows = came[:, 0]
    for k in range(1, quad):
        out_rows = out_rows + came[:, k]
    split = dot(collect, out_rows.reshape(experts * block, width), HIGHEST)
    for f in range(nx):
        moe = (
            first_weight * split[f * rows : (f + 1) * rows]
            + second_weight * split[(nx + f) * rows : (nx + f + 1) * rows]
        )
        r.moe_own[f] = moe
        r.moe_send[f] = moe.astype(BF16)
    moe_copies = []
    for n, step in enumerate(others):
        to = peer_x(step)
        moe_copies.append(
            remote(r.moe_send.at[to], r.moe_recv.at[n], r.moe_ss.at[n], r.moe_rs.at[n], (req, to))
        )
        moe_copies[n].start()

    for copy in part_copies + gain_copies + gath_copies + router_copies:
        copy.wait_send()
    for copy in list(near_copies.values()) + far_copies + core_copies:
        copy.wait_send()
    rest = r.rows_recv.at[pl.ds(0, chips - 1)]
    remote(rest, rest, r.disp_ss, r.disp_rs, (req, x)).wait_send()
    rest = r.back_recv.at[pl.ds(0, chips - 1)]
    remote(rest, rest, r.back_ss, r.back_rs, (req, x)).wait_send()

    for copy in moe_copies:
        copy.wait_recv()
    moe = r.moe_own[x]
    for n in range(nx - 1):
        moe = moe + r.moe_recv[n].astype(F32)
    r.layer_out[...] = (attended.astype(F32) + moe).astype(BF16)
    for copy in moe_copies:
        copy.wait_send()


def pass_on(a_in, b_in, a_out, b_out):
    a_out[...] = a_in[...]
    b_out[...] = b_in[...]


def shards(nz, ny, nx, resid, queries, new_keys, new_values, k_cache, v_cache, lengths, w_out,
           norm_gain, w_router, routes, w_gate, w_up, w_down):
    rows, width = resid.shape
    units = w_gate.shape[2]
    operands = (
        resid, queries, new_keys, new_values, k_cache, v_cache, lengths.reshape(1, rows), w_out,
        norm_gain.reshape(width // 128, 128), w_router.T, routes.T, w_gate[0], w_up[0], w_down[0],
    )
    scratch = plan(nz, ny, nx, rows, width, units, dict(zip(INPUTS, operands)))
    names = INPUTS + ["att_out", "layer_out"] + list(scratch)
    out = jax.ShapeDtypeStruct((rows, width), BF16)
    whole = pl.BlockSpec(memory_space=pltpu.VMEM)
    results = pl.pallas_call(
        functools.partial(kernel, nz, ny, nx, names),
        out_shape=(pltpu.VMEM((rows, width), BF16),) * 2,
        in_specs=[pl.BlockSpec(memory_space=pl.ANY)] * len(operands),
        out_specs=[whole] * 2,
        scratch_shapes=list(scratch.values()),
        compiler_params=pltpu.CompilerParams(
            collective_id=0, has_side_effects=True, vmem_limit_bytes=56 * 1024 * 1024
        ),
    )(*operands)
    return pl.pallas_call(
        pass_on, out_shape=(out, out), in_specs=[whole] * 2, out_specs=[whole] * 2
    )(*(pltpu.with_memory_space_constraint(a, pltpu.VMEM) for a in results))


def solution(mesh):
    nx = mesh.shape["tp"]
    nz = NZ
    ny = mesh.shape["req"] // (2 * nz)
    placed = (
        P("req", "tp"),
        P("req", "tp"),
        P("req", "tp"),
        P("req", "tp"),
        P("req", None, "tp"),
        P("req", None, "tp"),
        P("req"),
        P("tp", None),
        P("tp"),
        P("tp", None),
        P("req", None),
        P("req", "tp", None),
        P("req", "tp", None),
        P("req", None, "tp"),
    )
    return jax.shard_map(
        functools.partial(shards, nz, ny, nx),
        mesh=mesh,
        in_specs=placed,
        out_specs=(P("req", "tp"), P("req", "tp")),
        check_vma=False,
    )
```
